32 devices in a mesh: rows: 16 (over z, y, x), grp: 2 (over core).
Axes of the slice: x: 2, y: 2, z: 4, core: 2. Of those that a mesh axis runs over, the one named last changes fastest.
Arguments:
- start_basis: bfloat16 [16384, 64], P(('rows', 'grp')), may hold values from -6 to 6
- kernel_blocks: bfloat16 [2944, 256, 256], P(('rows', 'grp')), may hold values from -0.0390625 to 0.0390625
- block_row: int32 [2944], P(('rows', 'grp')), may hold values from 0 to 63, as said below
- block_col: int32 [2944], P(('rows', 'grp')), may hold values from 0 to 63, as said below
- block_count: int32 [32], P(('rows', 'grp')), may hold values from 1 to 92, as said below
Outputs:
- embedding: float32 [16384, 64], P(('rows', 'grp'))
- projected: float32 [64, 64], replicated
The draws below stay inside these ranges and needn't reach their ends.
Inputs may be any that keep to these rules, and one draw needn't show every extreme that they name: block_count[d] is the number of live slots of device d, its first ones; device 0 has all 92 live and the last device has 3. `block_row`: each slot's row block is one of its own device's 2 row blocks. `block_col`: each slot's column block is at least its row block; among one device's live slots at most 3 have their column block on any one device, the last device's live slots all lie on itself, and device 0 has a live slot whose column block lies on the last device.
All inputs are finite; a program needn't handle non-finite values.
Results may differ from the reference program's by a relative error of at most 0.0034.
Values may be sent and summed in bfloat16 or wider, within the bound.
A program may use at most 128 MiB of HBM per device.

```python
import jax
import jax.numpy as jnp
from jax import lax

B = 256
C = 64
ITERS = 2
RB_DEV = 2
SLOTS = 92
ROW_BLOCKS = 64
TOTAL_ROWS = 16384
TOTAL_SLOTS = 2944


def layout(key):
    devices = TOTAL_SLOTS // SLOTS
    device_ids = jnp.arange(devices, dtype=jnp.int32)
    base_count = (SLOTS * (devices - device_ids) + devices - 1) // devices
    cut_count = jax.random.randint(jax.random.fold_in(key, 11), (devices,), 0, max(1, SLOTS // 8) + 1)
    cut_count = jnp.where((device_ids == 0) | (device_ids == devices - 1), 0, cut_count)
    live_count = jnp.maximum(base_count - cut_count, 1)
    slot_ids = jnp.arange(SLOTS, dtype=jnp.int32)
    alive_mask = slot_ids[None, :] < live_count[:, None]
    random_keys = jax.random.randint(jax.random.fold_in(key, 12), (devices, SLOTS), 0, 1 << 19)
    scores = (jnp.where(alive_mask, 0, 1 << 20) + random_keys) * SLOTS + slot_ids[None, :]
    sort_order = jnp.argsort(scores, axis=1, stable=True)
    live_rank = jnp.argsort(sort_order, axis=1, stable=True).astype(jnp.int32)
    reach_span = devices - device_ids
    offset = jax.random.randint(jax.random.fold_in(key, 13), (devices,), 0, 1 << 20) % reach_span
    offset = jnp.where(device_ids == 0, devices - 1, offset)
    target_dev = device_ids[:, None] + (live_rank + offset[:, None]) % reach_span[:, None]
    row_local = jax.random.randint(jax.random.fold_in(key, 14), (devices, SLOTS), 0, RB_DEV)
    col_pick = jax.random.randint(jax.random.fold_in(key, 15), (devices, SLOTS), 0, 1 << 20)
    self_target = target_dev == device_ids[:, None]
    col_local = jnp.where(self_target, row_local + col_pick % (RB_DEV - row_local), col_pick % RB_DEV)
    row_ids = device_ids[:, None] * RB_DEV + row_local
    col_ids = target_dev * RB_DEV + col_local
    return (row_ids.reshape(-1).astype(jnp.int32), col_ids.reshape(-1).astype(jnp.int32), live_count.astype(jnp.int32))


def draw_block_row(key, part):
    return layout(key)[0]


def draw_block_col(key, part):
    return layout(key)[1]


def draw_block_count(key, part):
    return layout(key)[2]


def shard_levels(key, extent, shards, smallest, high):
    factor_of = 1.0
    for axis_at, blocks in shards:
        steps = jax.random.uniform(jax.random.fold_in(jax.random.fold_in(key, 6), axis_at), (blocks,), jnp.float32, smallest / len(shards), high / len(shards))
        factor_of = factor_of * jnp.repeat(jnp.exp(steps), extent[axis_at] // blocks).reshape((-1,) + (1,) * (len(extent) - 1 - axis_at))
    return factor_of


def centred(rng, dims, deviation, bound, pieces=(), kind=jnp.bfloat16):
    entries = deviation * jax.random.normal(rng, dims, jnp.float32)
    if pieces:
        entries = entries * shard_levels(rng, dims, pieces, -0.22, 0.18)
    return jnp.clip(entries, -bound, bound).astype(kind)


def setup_inputs(seed: int = 0) -> dict:
    streams_of = jax.random.split(jax.random.key(seed), 6)
    start_basis = centred(streams_of[0], (TOTAL_ROWS, C), 1.0, 6.0, ((0, 32),))
    kernel_blocks = centred(streams_of[1], (TOTAL_SLOTS, B, B), (B * SLOTS) ** -0.5, 0.0390625, ((0, 32),))
    block_row = draw_block_row(jax.random.fold_in(streams_of[5], 71), 0)
    block_col = draw_block_col(jax.random.fold_in(streams_of[5], 71), 0)
    block_count = draw_block_count(jax.random.fold_in(streams_of[5], 71), 0)
    return dict(start_basis=start_basis, kernel_blocks=kernel_blocks, block_row=block_row, block_col=block_col, block_count=block_count)


def image_of(kernel_blocks, block_row, block_col, block_count, basis):
    devices = TOTAL_SLOTS // SLOTS
    basis_tiles = basis.reshape(ROW_BLOCKS, B, C)
    stacked = kernel_blocks.reshape(devices, SLOTS, B, B)
    row_lists = block_row.reshape(devices, SLOTS)
    col_lists = block_col.reshape(devices, SLOTS)

    def visit(running, inputs):
        blocks, row_ids, col_ids, live_total = inputs
        alive_mask = (jnp.arange(SLOTS, dtype=jnp.int32) < live_total).astype(jnp.float32)[:, None, None]
        blocks_wide = blocks.astype(jnp.float32)
        forward = jnp.einsum('sij,sjc->sic', blocks_wide, basis_tiles[col_ids].astype(jnp.float32), precision=lax.Precision.HIGHEST)
        mirrored = jnp.einsum('sji,sjc->sic', blocks_wide, basis_tiles[row_ids].astype(jnp.float32), precision=lax.Precision.HIGHEST).astype(jnp.bfloat16)
        mirrored = lax.optimization_barrier(mirrored).astype(jnp.float32)
        running = running.at[row_ids].add(forward * alive_mask).at[col_ids].add(mirrored * alive_mask)
        return (running, None)
    running, _ = lax.scan(visit, jnp.zeros((ROW_BLOCKS, B, C), jnp.float32), (stacked, row_lists, col_lists, block_count))
    return running.reshape(TOTAL_ROWS, C)

def reference(start_basis, kernel_blocks, block_row, block_col, block_count):
    basis = start_basis
    result = None
    projected = None
    for iteration in range(ITERS):
        image_rows = image_of(kernel_blocks, block_row, block_col, block_count, basis)
        gram_part = jnp.dot(image_rows.T, image_rows, precision=lax.Precision.HIGHEST) / TOTAL_ROWS
        if iteration == ITERS - 1:
            projected = jnp.dot(basis.astype(jnp.float32).T, image_rows, precision=lax.Precision.HIGHEST) / TOTAL_ROWS
        lower_factor = jnp.linalg.cholesky(gram_part)
        inverse = jax.scipy.linalg.solve_triangular(lower_factor, jnp.eye(C, dtype=jnp.float32), lower=True)
        result = jnp.dot(image_rows, inverse.T, precision=lax.Precision.HIGHEST)
        basis = result.astype(jnp.bfloat16)
    return (result, projected)
```

```python
import functools

import jax
import jax.numpy as jnp
from jax import lax
from jax.experimental import pallas as pl
from jax.experimental.pallas import tpu as pltpu
from jax.sharding import PartitionSpec as P

ITERS = 2
PLANE = 4
KINDS = 2
MESH = pl.DeviceIdType.MESH
HIGH = lax.Precision.HIGHEST
CHUNKS = 4


def split_even(total, parts):
    edges = [total * i // parts for i in range(parts + 1)]
    return list(zip(edges[:-1], edges[1:]))


def nt_dot(a, b, precision=None):
    return lax.dot_general(
        a, b, (((1,), (1,)), ((), ())), preferred_element_type=jnp.float32, precision=precision
    )


def inverse_factor(gram, columns):
    row_id = lax.broadcasted_iota(jnp.int32, (columns, 2 * columns), 0)
    lane_id = lax.broadcasted_iota(jnp.int32, (columns, 2 * columns), 1)
    unit = jnp.where(lane_id == row_id + columns, 1.0, 0.0).astype(jnp.float32)
    work = jnp.where(lane_id < columns, gram, unit)
    for k in range(columns):
        factor = work[:, k : k + 1] * (1.0 / work[k : k + 1, k : k + 1])
        work = jnp.where(row_id > k, work - factor * work[k : k + 1, :], work)
    pivots = jnp.sum(jnp.where(lane_id == row_id, work, 0.0), axis=1, keepdims=True)
    guess = lax.rsqrt(pivots)
    scale = guess * (1.5 - 0.5 * (pivots * guess) * guess)
    return work[:, columns:] * scale


def fold(square):
    half = square.shape[0] // 2
    return jnp.concatenate([square[:half], square[half:]], axis=1)


def unfold(packed):
    half = packed.shape[1] // 2
    return jnp.concatenate([packed[:, :half], packed[:, half:]], axis=0)


def kernel(
    planes, total_rows, per_peer,
    code, start_ref, blocks_hbm, embed_ref, proj_ref, inverse_ref,
    blocks, turned, gathered, pair_send, pair_recv, mate_send, mate_recv,
    up_send, up_recv, far_send, far_recv, column, own_sum, image, line, line_recv,
    load_sem, ag_z_s, ag_z_r, ag_p_s, ag_p_r, ag_d_s, ag_d_r, ag_c_s, ag_c_r,
    rs_c_s, rs_c_r, rs_p_s, rs_p_r, rs_u_s, rs_u_r, rs_z_s, rs_z_r, ar_s, ar_r,
):
    columns, size = gathered.shape[1:]
    slots = blocks.shape[0]
    rows_at = lax.axis_index("rows")
    c = lax.axis_index("grp")
    z = rows_at // PLANE
    p = rows_at % PLANE
    px, py = p % 2, p // 2

    def mate(q):
        x = px + (q % 2) * (1 - 2 * px)
        y = py + (q // 2) * (1 - 2 * py)
        return 2 * y + x

    mates = [mate(q) for q in range(PLANE)]

    def number(zz, pp, cc):
        return ((zz * PLANE + pp) * 2 + cc)

    def unit(zz, pp, cc):
        return gathered.at[pl.ds(number(zz, pp, cc) * KINDS, KINDS)]

    def remote(src, dst, s, r, zz, pp, cc):
        return pltpu.make_async_remote_copy(
            src, dst, s, r, device_id=(zz * PLANE + pp, cc), device_id_type=MESH
        )

    loads = [
        pltpu.make_async_copy(
            blocks_hbm.at[pl.ds(lo, hi - lo)], blocks.at[pl.ds(lo, hi - lo)], load_sem.at[i]
        )
        for i, (lo, hi) in enumerate(split_even(slots, CHUNKS))
    ]
    for copy in loads:
        copy.start()
    barrier = pltpu.get_barrier_semaphore()
    greeted = [(z, mates[q], 1 - c if f else c) for q in range(PLANE) for f in (0, 1) if q or f]
    greeted += [((z + s) % planes, p, c) for s in range(1, planes)]
    for zz, pp, cc in greeted:
        pl.semaphore_signal(barrier, inc=1, device_id=(zz * PLANE + pp, cc), device_id_type=MESH)
    pl.semaphore_wait(barrier, len(greeted))

    def above(dz):
        return z + dz < planes

    def below(dz):
        return z - dz >= 0

    own_at = number(z, p, c) * KINDS

    def when(condition):
        return pl.when(condition)

    def g_far(dz):
        return remote(unit(z, p, c), unit(z, p, c), ag_z_s.at[dz], ag_z_r.at[dz], z - dz, p, c)

    def g_far_in(dz):
        at = unit(z + dz, p, c)
        return remote(at, at, ag_z_s.at[dz], ag_z_r.at[dz], z + dz, p, c)

    def g_mate(dz, q):
        at, i = unit(z + dz, p, c), dz * 3 + q - 1
        return remote(at, at, ag_p_s.at[i], ag_p_r.at[i], z, mates[q], c)

    def g_mate_in(dz, q):
        at, i = unit(z + dz, mates[q], c), dz * 3 + q - 1
        return remote(at, at, ag_p_s.at[i], ag_p_r.at[i], z, mates[q], c)

    def g_down(q):
        at = unit(z, mates[q], c)
        return remote(at, at, ag_d_s.at[q], ag_d_r.at[q], z - 1, p, c)

    def g_down_in(q):
        at = unit(z + 1, mates[q], c)
        return remote(at, at, ag_d_s.at[q], ag_d_r.at[q], z + 1, p, c)

    def g_core(dz, q):
        at, i = unit(z + dz, mates[q], c), dz * PLANE + q
        return remote(at, at, ag_c_s.at[i], ag_c_r.at[i], z, p, 1 - c)

    def g_core_in(dz, q):
        at, i = unit(z + dz, mates[q], 1 - c), dz * PLANE + q
        return remote(at, at, ag_c_s.at[i], ag_c_r.at[i], z, p, 1 - c)

    def down_to(q):
        return (z > 0) | (mates[q] < p)

    def up_to(q):
        return (z > 0) | (mates[q] > p)

    def r_pair(dz):
        span = pl.ds(dz * PLANE, PLANE)
        return remote(
            pair_send.at[span], pair_recv.at[span], rs_c_s.at[dz], rs_c_r.at[dz], z, p, 1 - c
        )

    def r_mate(dz, q):
        i = dz * 3 + q - 1
        return remote(
            mate_send.at[i], mate_recv.at[i], rs_p_s.at[i], rs_p_r.at[i], z, mates[q], c
        )

    def r_up():
        return remote(up_send, up_recv, rs_u_s.at[0], rs_u_r.at[0], z + 1, p, c)

    def r_far(dz):
        return remote(
            far_send.at[dz], far_recv.at[dz], rs_z_s.at[dz], rs_z_r.at[dz], z + dz, p, c
        )

    def decode(word):
        return word // 8, (word // 4) % 2, (word // 2) % 2, word % 2

    def mirror_sums(device):
        low, high = gathered[own_at], gathered[own_at + 1]
        sums = [jnp.zeros((columns, size), jnp.float32) for _ in range(KINDS)]
        for j in range(per_peer):
            slot, row, col, live = decode(code[device * per_peer + j])
            left = lax.select(row == 1, high, low)
            product = jnp.dot(left, blocks[slot], preferred_element_type=jnp.float32)
            sums[0] = sums[0] + product * (live * (1 - col)).astype(jnp.float32)
            sums[1] = sums[1] + product * (live * col).astype(jnp.float32)
        return sums

    def give(dz):
        def one(pp, _):
            sums = mirror_sums(number(z + dz, pp, 1 - c))
            for kind in range(KINDS):
                pair_send[dz * PLANE + pp, kind] = sums[kind].astype(jnp.bfloat16)
            return 0

        lax.fori_loop(0, PLANE, one, 0)
        r_pair(dz).start()

    def keep(dz):
        r_pair(dz).wait_recv()
        for q in range(PLANE):
            pp = mates[q]
            sums = mirror_sums(number(z + dz, pp, c))
            for kind in range(KINDS):
                value = sums[kind] + pair_recv[dz * PLANE + pp, kind].astype(jnp.float32)
                if dz == 0:
                    own_sum[q, kind] = value
                elif dz == 1:
                    up_send[q, kind] = value.astype(jnp.bfloat16)
                elif q == 0:
                    column[dz, kind] = value
                else:
                    mate_send[dz * 3 + q - 1, kind] = value.astype(jnp.bfloat16)
            if dz >= 2 and q:
                r_mate(dz, q).start()
        if dz == 1:
            r_up().start()

    def send_own():
        for q in range(1, PLANE):

            @when(up_to(q))
            def _(q=q):
                for kind in range(KINDS):
                    mate_send[q - 1, kind] = own_sum[q, kind].astype(jnp.bfloat16)
                r_mate(0, q).start()

    def pass_far(dz):
        total = [column[dz, kind] for kind in range(KINDS)]
        for q in range(1, PLANE):
            r_mate(dz, q).wait_recv()
            for kind in range(KINDS):
                total[kind] = total[kind] + mate_recv[dz * 3 + q - 1, kind].astype(jnp.float32)
        for kind in range(KINDS):
            far_send[dz, kind] = total[kind].astype(jnp.bfloat16)
        r_far(dz).start()

    def forward(dz):
        def one(pp, _):
            @when((z + dz > 0) | (pp >= p))
            def _():
                sums = [jnp.zeros((columns, size), jnp.float32) for _ in range(KINDS)]
                for cc in range(2):
                    device = number(z + dz, pp, cc)
                    low, high = gathered[device * KINDS], gathered[device * KINDS + 1]
                    for j in range(per_peer):
                        slot, row, col, live = decode(code[device * per_peer + j])
                        left = lax.select(col == 1, high, low)
                        product = jnp.dot(left, turned[slot], preferred_element_type=jnp.float32)
                        sums[0] = sums[0] + product * (live * (1 - row)).astype(jnp.float32)
                        sums[1] = sums[1] + product * (live * row).astype(jnp.float32)
                for kind in range(KINDS):
                    image[kind] = image[kind] + sums[kind]

            return 0

        lax.fori_loop(0, PLANE, one, 0)

    def turn(lo, hi):
        def one(slot, _):
            turned[slot] = blocks[slot].T
            return 0

        lax.fori_loop(lo, hi, one, 0)

    turns = split_even(slots, 4)
    far = list(range(planes - 1, 1, -1))

    for iteration in range(ITERS):
        last = iteration == ITERS - 1
        if iteration == 0:
            for kind in range(KINDS):
                gathered[own_at + kind] = start_ref[:, kind * size : (kind + 1) * size]
        for dz in far + [1]:
            when(below(dz))(lambda dz=dz: g_far(dz).start())
        for q in (3, 1, 2):
            when(down_to(q))(lambda q=q: g_mate(0, q).start())
        g_core(0, 0).start()
        image[...] = jnp.zeros_like(image)
        if iteration == 0:
            for copy in loads:
                copy.wait()
        for dz in far + [1, 0]:
            when(above(dz))(lambda dz=dz: give(dz))
        for dz in far + [1, 0]:
            when(above(dz))(lambda dz=dz: keep(dz))
        when(z == 0)(send_own)
        if iteration == 0:
            turn(*turns[0])

        for dz in range(1, planes):

            @when(above(dz))
            def _(dz=dz):
                g_far_in(dz).wait_recv()
                if dz >= 2:
                    for q in (3, 1, 2):
                        g_mate(dz, q).start()
                g_core(dz, 0).start()

        for q in range(1, PLANE):

            @when(up_to(q))
            def _(q=q):
                g_mate_in(0, q).wait_recv()
                g_core(0, q).start()

                @when(z > 0)
                def _():
                    g_down(q).start()

        if iteration == 0:
            turn(*turns[1])
        for dz in far:
            when(above(dz))(lambda dz=dz: pass_far(dz))

        @when(z > 0)
        def _():
            r_up().wait_recv()
            for q in range(PLANE):
                for kind in range(KINDS):
                    own_sum[q, kind] = own_sum[q, kind] + up_recv[q, kind].astype(jnp.float32)
            send_own()

        if iteration == 0:
            turn(*turns[2])
            turn(*turns[3])
        g_core_in(0, 0).wait_recv()
        for q in range(1, PLANE):
            when(up_to(q))(lambda q=q: g_core_in(0, q).wait_recv())
        forward(0)

        if planes > 1:

            @when(above(1))
            def _():
                for q in range(1, PLANE):
                    g_down_in(q).wait_recv()
                    g_core(1, q).start()
                for q in range(PLANE):
                    g_core_in(1, q).wait_recv()
                forward(1)

        for dz in range(2, planes):

            @when(above(dz))
            def _(dz=dz):
                for q in range(1, PLANE):
                    g_mate_in(dz, q).wait_recv()
                    g_core(dz, q).start()

        for dz in range(2, planes):

            @when(above(dz))
            def _(dz=dz):
                for q in range(PLANE):
                    g_core_in(dz, q).wait_recv()
                forward(dz)

        for kind in range(KINDS):
            image[kind] = image[kind] + own_sum[0, kind]
        for q in range(1, PLANE):

            @when(down_to(q))
            def _(q=q):
                r_mate(0, q).wait_recv()
                for kind in range(KINDS):
                    image[kind] = image[kind] + mate_recv[q - 1, kind].astype(jnp.float32)

        for dz in range(2, planes):

            @when(below(dz))
            def _(dz=dz):
                r_far(dz).wait_recv()
                for kind in range(KINDS):
                    image[kind] = image[kind] + far_recv[dz, kind].astype(jnp.float32)

        for dz in range(1, planes):
            when(below(dz))(lambda dz=dz: g_far(dz).wait_send())
        for q in range(1, PLANE):
            when(down_to(q))(lambda q=q: g_mate(0, q).wait_send())
            when(up_to(q))(lambda q=q: r_mate(0, q).wait_send())
            when(up_to(q))(lambda q=q: g_core(0, q).wait_send())
            when(z > 0)(lambda q=q: g_down(q).wait_send())
        g_core(0, 0).wait_send()
        r_pair(0).wait_send()
        for dz in range(1, planes):

            @when(above(dz))
            def _(dz=dz):
                r_pair(dz).wait_send()
                for q in range(PLANE):
                    g_core(dz, q).wait_send()
                if dz == 1:
                    r_up().wait_send()
                else:
                    for q in range(1, PLANE):
                        g_mate(dz, q).wait_send()
                        r_mate(dz, q).wait_send()
                    r_far(dz).wait_send()

        gram = jnp.zeros((columns, columns), jnp.float32)
        projection = jnp.zeros((columns, columns), jnp.float32)
        for kind in range(KINDS):
            rows = image[kind]
            gram = gram + nt_dot(rows, rows, HIGH)
            if last:
                old = gathered[own_at + kind].astype(jnp.float32)
                projection = projection + nt_dot(old, rows, HIGH)
        half = columns // 2
        tall = columns if last else half
        peers = 2 * PLANE - 1
        base = iteration * 2
        rbase = iteration * (peers + planes - 1)
        sbase = iteration * (peers + 2 * planes)
        line[base, :half] = fold(gram)
        if last:
            line[base, half:] = fold(projection)
        copies = []
        for i, (zz, pp, cc) in enumerate(greeted[:peers]):
            copies.append(
                remote(
                    line.at[base, pl.ds(0, tall)], line_recv.at[rbase + i, pl.ds(0, tall)],
                    ar_s.at[sbase + i], ar_r.at[sbase + i], zz, pp, cc,
                )
            )
        for copy in copies:
            copy.start()
        total = line[base, :tall]
        for i, copy in enumerate(copies):
            copy.wait()
            total = total + line_recv[rbase + i, :tall]
        line[base + 1, :tall] = total
        parts = [[], []]
        for part in range(2 if last else 1):
            span = pl.ds(part * half, half)
            for s in range(1, planes):
                at = sbase + peers + part * planes + s
                copy = remote(
                    line.at[base + 1, span], line_recv.at[rbase + peers + s - 1, span],
                    ar_s.at[at], ar_r.at[at], (z + s) % planes, p, c,
                )
                copy.start()
                parts[part].append(copy)
        for copy in parts[0]:
            copy.wait()
        whole = line[base + 1, :half]
        for s in range(1, planes):
            whole = whole + line_recv[rbase + peers + s - 1, :half]
        whole = unfold(whole / total_rows)
        inverse = inverse_factor(jnp.concatenate([whole, whole], axis=1), columns)
        if last:
            inverse_ref[...] = inverse
            for copy in parts[1]:
                copy.wait()
            whole = line[base + 1, half:]
            for s in range(1, planes):
                whole = whole + line_recv[rbase + peers + s - 1, half:]
            proj_ref[...] = unfold(whole)
        for kind in range(KINDS):
            if last:
                embed_ref[:, kind * size : (kind + 1) * size] = image[kind]
            else:
                result = jnp.dot(
                    inverse, image[kind], precision=HIGH, preferred_element_type=jnp.float32
                )
                gathered[own_at + kind] = result.astype(jnp.bfloat16)


def on_device(start_basis, kernel_blocks, block_row, block_col, block_count):
    devices = lax.axis_size("rows") * lax.axis_size("grp")
    me = lax.axis_index("rows") * lax.axis_size("grp") + lax.axis_index("grp")
    slots, size, _ = kernel_blocks.shape
    own_rows, columns = start_basis.shape
    per_peer = (slots + devices - 1) // devices
    planes = lax.axis_size("rows") // PLANE
    total_rows = own_rows * devices

    positions = jnp.arange(slots, dtype=jnp.int32)
    alive = positions < block_count[0]
    local_row = jnp.clip(block_row - me * KINDS, 0, KINDS - 1)
    target = block_col // KINDS
    earlier = (
        (target[:, None] == target[None, :])
        & alive[None, :]
        & (positions[None, :] < positions[:, None])
    )
    rank = jnp.sum(earlier.astype(jnp.int32), axis=1)
    spot = jnp.where(alive, target * per_peer + rank, -1)
    hit = spot[None, :] == jnp.arange(devices * per_peer, dtype=jnp.int32)[:, None]
    word = positions * 8 + local_row * 4 + (block_col - target * KINDS) * 2 + 1
    code = jnp.sum(jnp.where(hit, word[None, :], 0), axis=1)

    smem = pl.BlockSpec(memory_space=pltpu.SMEM)
    vmem = pl.BlockSpec(memory_space=pltpu.VMEM)
    half = pltpu.VMEM
    dma = pltpu.SemaphoreType.DMA
    peers = 2 * PLANE - 1

    def halves(*lead):
        return pltpu.VMEM((*lead, KINDS, columns, size), jnp.bfloat16)

    def singles(*lead):
        return pltpu.VMEM((*lead, KINDS, columns, size), jnp.float32)

    arounds = ITERS * (peers + 2 * planes)
    image, projected, inverse = pl.pallas_call(
        functools.partial(kernel, planes, total_rows, per_peer),
        out_shape=(
            jax.ShapeDtypeStruct((columns, own_rows), jnp.float32),
            jax.ShapeDtypeStruct((columns, columns), jnp.float32),
            jax.ShapeDtypeStruct((columns, columns), jnp.float32),
        ),
        in_specs=[smem, vmem, pl.BlockSpec(memory_space=pl.ANY)],
        out_specs=(vmem, vmem, vmem),
        scratch_shapes=[
            pltpu.VMEM((slots, size, size), jnp.bfloat16),
            pltpu.VMEM((slots, size, size), jnp.bfloat16),
            pltpu.VMEM((devices * KINDS, columns, size), jnp.bfloat16),
            halves(planes * PLANE),
            halves(planes * PLANE),
            halves(planes * 3),
            halves(planes * 3),
            halves(PLANE),
            halves(PLANE),
            halves(planes),
            halves(planes),
            singles(planes),
            singles(PLANE),
            singles(),
            pltpu.VMEM((ITERS * 2, columns, 2 * columns), jnp.float32),
            pltpu.VMEM((ITERS * (peers + planes - 1), columns, 2 * columns), jnp.float32),
            dma((CHUNKS,)),
            dma((planes,)), dma((planes,)),
            dma((planes * 3,)), dma((planes * 3,)),
            dma((PLANE,)), dma((PLANE,)),
            dma((planes * PLANE,)), dma((planes * PLANE,)),
            dma((planes,)), dma((planes,)),
            dma((planes * 3,)), dma((planes * 3,)),
            dma((1,)), dma((1,)),
            dma((planes,)), dma((planes,)),
            dma((arounds,)), dma((arounds,)),
        ],
        compiler_params=pltpu.CompilerParams(
            collective_id=0, has_side_effects=True, vmem_limit_bytes=62 * 1024 * 1024
        ),
    )(code, start_basis.T, kernel_blocks)
    embedded = lax.dot_general(image, inverse, (((0,), (1,)), ((), ())), precision=HIGH)
    return embedded, projected / total_rows


def solution(mesh):
    in_specs = (
        P(("rows", "grp"), None),
        P(("rows", "grp"), None, None),
        P(("rows", "grp")),
        P(("rows", "grp")),
        P(("rows", "grp")),
    )
    out_specs = (P(("rows", "grp"), None), P())
    return jax.shard_map(
        on_device, mesh=mesh, in_specs=in_specs, out_specs=out_specs, check_vma=False
    )
```

```python
import functools

import jax
import jax.numpy as jnp
from jax import lax
from jax.experimental import pallas as pl
from jax.experimental.pallas import tpu as pltpu
from jax.sharding import PartitionSpec as P

ITERS = 2
PLANE = 4
KINDS = 2
MESH = pl.DeviceIdType.MESH
HIGH = lax.Precision.HIGHEST
CHUNKS = 4


def split_even(total, parts):
    edges = [total * i // parts for i in range(parts + 1)]
    return list(zip(edges[:-1], edges[1:]))


def nt_dot(a, b, precision=None):
    return lax.dot_general(
        a, b, (((1,), (1,)), ((), ())), preferred_element_type=jnp.float32, precision=precision
    )


def inverse_root(value):
    guess = lax.rsqrt(value)
    return guess * (1.5 - 0.5 * (value * guess) * guess)


def inverse_factor(gram, columns):
    tall = 8
    wide = 2 * columns
    row_id = lax.broadcasted_iota(jnp.int32, (columns, wide), 0)
    lane_id = lax.broadcasted_iota(jnp.int32, (columns, wide), 1)
    both = jnp.concatenate([gram, gram], axis=1)
    on_diagonal = (lane_id == row_id) | (lane_id == row_id + columns)
    diagonal = jnp.where(on_diagonal, both, 0.0)
    across = inverse_root(jnp.sum(diagonal, axis=0, keepdims=True))
    down = inverse_root(0.5 * jnp.sum(diagonal, axis=1, keepdims=True))
    unit = jnp.where(lane_id == row_id + columns, 1.0, 0.0).astype(jnp.float32)
    work = jnp.where(lane_id < columns, both * down * across, unit)
    tiles = [work[i : i + tall] for i in range(0, columns, tall)]

    def spread(row):
        return jnp.broadcast_to(row, (tall, wide))

    done = []
    for t in range(len(tiles)):
        k = t * tall
        cols = [
            [jnp.broadcast_to(tile[:, k + j : k + j + 1], (tall, wide)) for tile in tiles[t:]]
            for j in range(tall)
        ]
        rows = [spread(tiles[t][i : i + 1]) for i in range(tall)]
        p = [[spread(cols[j][0][i : i + 1]) for j in range(i + 1)] for i in range(tall)]
        inv = [None] * tall
        for j in range(0, tall, 2):
            det = p[j][j] * p[j + 1][j + 1] - p[j + 1][j] * p[j + 1][j]
            inv[j] = 1.0 / p[j][j]
            inv[j + 1] = p[j][j] * (1.0 / det)
            lead = p[j + 1][j] * inv[j]
            rows[j + 1] = rows[j + 1] - lead * rows[j]
            cols[j + 1] = [c1 - lead * c0 for c1, c0 in zip(cols[j + 1], cols[j])]
            p[j + 1][j + 1] = p[j + 1][j + 1] - lead * p[j + 1][j]
            for i in range(j + 2, tall):
                p[i][j + 1] = p[i][j + 1] - lead * p[i][j]
            for i in range(j + 2, tall):
                l0, l1 = p[i][j] * inv[j], p[i][j + 1] * inv[j + 1]
                rows[i] = rows[i] - l0 * rows[j] - l1 * rows[j + 1]
                cols[i] = [
                    ci - l0 * c0 - l1 * c1 for ci, c0, c1 in zip(cols[i], cols[j], cols[j + 1])
                ]
                for m in range(i, tall):
                    p[m][i] = p[m][i] - l0 * p[m][j] - l1 * p[m][j + 1]
        for i in range(tall):
            done.append((rows[i] * inverse_root(p[i][i]))[:1])
        scaled = [rows[i] * inv[i] for i in range(tall)]
        for at in range(t + 1, len(tiles)):
            for i in range(tall):
                tiles[at] = tiles[at] - cols[i][at - t] * scaled[i]
    return (jnp.concatenate(done, axis=0) * across)[:, columns:]


def fold(square):
    half = square.shape[0] // 2
    return jnp.concatenate([square[:half], square[half:]], axis=1)


def unfold(packed):
    half = packed.shape[1] // 2
    return jnp.concatenate([packed[:, :half], packed[:, half:]], axis=0)


def kernel(
    planes, total_rows, per_peer, columns,
    code, start_ref, blocks_hbm, embed_ref, proj_ref, inverse_ref,
    blocks, turned, gathered, pair_send, pair_recv, mate_send, mate_recv,
    up_send, up_recv, far_send, far_recv, column, own_sum, forward_sum, image, line, line_recv,
    load_sem, ag_z_s, ag_z_r, ag_p_s, ag_p_r, ag_d_s, ag_d_r, ag_c_s, ag_c_r,
    rs_c_s, rs_c_r, rs_p_s, rs_p_r, rs_u_s, rs_u_r, rs_z_s, rs_z_r, ar_s, ar_r,
):
    size, both = gathered.shape[1:]
    slots = blocks.shape[0]
    rows_at = lax.axis_index("rows")
    c = lax.axis_index("grp")
    z = rows_at // PLANE
    p = rows_at % PLANE
    px, py = p % 2, p // 2

    def mate(q):
        x = px + (q % 2) * (1 - 2 * px)
        y = py + (q // 2) * (1 - 2 * py)
        return 2 * y + x

    mates = [mate(q) for q in range(PLANE)]
    others = (3, 1, 2)

    def number(zz, pp, cc):
        return (zz * PLANE + pp) * 2 + cc

    def remote(src, dst, s, r, zz, pp, cc):
        return pltpu.make_async_remote_copy(
            src, dst, s, r, device_id=(zz * PLANE + pp, cc), device_id_type=MESH
        )

    loads = [
        pltpu.make_async_copy(
            blocks_hbm.at[pl.ds(lo, hi - lo)], blocks.at[pl.ds(lo, hi - lo)], load_sem.at[i]
        )
        for i, (lo, hi) in enumerate(split_even(slots, CHUNKS))
    ]
    for copy in loads:
        copy.start()
    barrier = pltpu.get_barrier_semaphore()
    greeted = [(z, mates[q], 1 - c if f else c) for q in range(PLANE) for f in (0, 1) if q or f]
    greeted += [((z + s) % planes, p, c) for s in range(1, planes)]
    for zz, pp, cc in greeted:
        pl.semaphore_signal(barrier, inc=1, device_id=(zz * PLANE + pp, cc), device_id_type=MESH)
    pl.semaphore_wait(barrier, len(greeted))

    def above(dz):
        return z + dz < planes

    def below(dz):
        return z - dz >= 0

    when = pl.when
    me = number(z, p, c)

    def whole(device):
        return gathered.at[device]

    def part(device, h):
        return gathered.at[device, pl.ds(h * (size // 2), size // 2)]

    def g_next():
        at = whole(me)
        return remote(at, at, ag_z_s.at[0], ag_z_r.at[0], z - 1, p, c)

    def g_next_in():
        at = whole(number(z + 1, p, c))
        return remote(at, at, ag_z_s.at[0], ag_z_r.at[0], z + 1, p, c)

    def g_far(dz, h):
        at, i = part(me, h), dz * 2 + h
        return remote(at, at, ag_z_s.at[i], ag_z_r.at[i], z - dz, p, c)

    def g_far_in(dz, h):
        at, i = part(number(z + dz, p, c), h), dz * 2 + h
        return remote(at, at, ag_z_s.at[i], ag_z_r.at[i], z + dz, p, c)

    def g_own(q):
        at = whole(me)
        return remote(at, at, ag_p_s.at[q], ag_p_r.at[q], z, mates[q], c)

    def g_own_in(q):
        at = whole(number(z, mates[q], c))
        return remote(at, at, ag_p_s.at[q], ag_p_r.at[q], z, mates[q], c)

    def g_mate(dz, q, h):
        at, i = part(number(z + dz, p, c), h), (dz * PLANE + q) * 2 + h
        return remote(at, at, ag_p_s.at[i], ag_p_r.at[i], z, mates[q], c)

    def g_mate_in(dz, q, h):
        at, i = part(number(z + dz, mates[q], c), h), (dz * PLANE + q) * 2 + h
        return remote(at, at, ag_p_s.at[i], ag_p_r.at[i], z, mates[q], c)

    def g_down(q):
        at = whole(number(z, mates[q], c))
        return remote(at, at, ag_d_s.at[q], ag_d_r.at[q], z - 1, p, c)

    def g_down_in(q):
        at = whole(number(z + 1, mates[q], c))
        return remote(at, at, ag_d_s.at[q], ag_d_r.at[q], z + 1, p, c)

    def g_core(dz, q):
        at, i = whole(number(z + dz, mates[q], c)), dz * PLANE + q
        return remote(at, at, ag_c_s.at[i], ag_c_r.at[i], z, p, 1 - c)

    def g_core_in(dz, q):
        at, i = whole(number(z + dz, mates[q], 1 - c)), dz * PLANE + q
        return remote(at, at, ag_c_s.at[i], ag_c_r.at[i], z, p, 1 - c)

    def down_to(q):
        return (z > 0) | (mates[q] < p)

    def up_to(q):
        return (z > 0) | (mates[q] > p)

    def r_pair(dz):
        span = pl.ds(dz * PLANE, PLANE)
        return remote(
            pair_send.at[span], pair_recv.at[span], rs_c_s.at[dz], rs_c_r.at[dz], z, p, 1 - c
        )

    def r_own(q):
        return remote(
            mate_send.at[q], mate_recv.at[q], rs_p_s.at[q], rs_p_r.at[q], z, mates[q], c
        )

    def r_mate(dz, q, h):
        i = (dz * PLANE + q) * 2 + h
        at = (dz * PLANE + q, pl.ds(h * columns, columns))
        return remote(
            mate_send.at[at], mate_recv.at[at], rs_p_s.at[i], rs_p_r.at[i], z, mates[q], c
        )

    def r_up(q):
        return remote(up_send.at[q], up_recv.at[q], rs_u_s.at[q], rs_u_r.at[q], z + 1, p, c)

    def r_far(dz, h):
        i = dz * 2 + h
        at = (dz, pl.ds(h * columns, columns))
        return remote(far_send.at[at], far_recv.at[at], rs_z_s.at[i], rs_z_r.at[i], z + dz, p, c)

    def decode(word):
        return word // 8, (word // 4) % 2, (word // 2) % 2, word % 2

    nothing = jnp.zeros((columns, size), jnp.bfloat16)

    def mirror_sums(device):
        sums = None
        for j in range(per_peer):
            slot, row, col, live = decode(code[device * per_peer + j])
            rows = lax.select(row == 1, turned[columns:], turned[:columns])
            left = jnp.concatenate(
                [
                    lax.select(live * (1 - col) == 1, rows, nothing),
                    lax.select(live * col == 1, rows, nothing),
                ],
                axis=0,
            )
            product = jnp.dot(left, blocks[slot], preferred_element_type=jnp.float32)
            sums = product if sums is None else sums + product
        return sums

    def give(dz):
        for pp in range(PLANE):
            pair_send[dz * PLANE + pp] = mirror_sums(number(z + dz, pp, 1 - c)).astype(
                jnp.bfloat16
            )
        r_pair(dz).start()

    def keep(dz):
        r_pair(dz).wait_recv()
        for q in others + (0,):
            pp = mates[q]
            value = mirror_sums(number(z + dz, pp, c)) + pair_recv[dz * PLANE + pp].astype(
                jnp.float32
            )
            if dz == 0:
                own_sum[q] = value
            elif dz == 1:
                up_send[q] = value.astype(jnp.bfloat16)
                r_up(q).start()
            elif q == 0:
                column[dz] = value
            else:
                mate_send[dz * PLANE + q] = value.astype(jnp.bfloat16)
        if dz >= 2:
            for h in range(2):
                for q in others:
                    r_mate(dz, q, h).start()

    def send_own(q):
        mate_send[q] = own_sum[q].astype(jnp.bfloat16)
        r_own(q).start()

    def pass_far(dz, h):
        at = pl.ds(h * columns, columns)
        total = column[dz, at]
        for q in others:
            r_mate(dz, q, h).wait_recv()
            total = total + mate_recv[dz * PLANE + q, at].astype(jnp.float32)
        far_send[dz, at] = total.astype(jnp.bfloat16)
        r_far(dz, h).start()

    lane = lax.broadcasted_iota(jnp.int32, (size, both), 1)
    sides = [
        jnp.where((lane >= columns) == bool(kind), 1.0, 0.0).astype(jnp.bfloat16)
        for kind in range(KINDS)
    ]
    neither = jnp.zeros((size, both), jnp.bfloat16)

    def forward_sums(zz, pp):
        sums = None
        for cc in range(2):
            device = number(zz, pp, cc)
            straight = gathered[device]
            crossed = jnp.concatenate([straight[:, columns:], straight[:, :columns]], axis=1)
            for j in range(per_peer):
                slot, row, col, live = decode(code[device * per_peer + j])
                side = lax.select(
                    live * (1 - row) == 1,
                    sides[0],
                    lax.select(live * row == 1, sides[1], neither),
                )
                right = lax.select(row == col, straight, crossed) * side
                product = jnp.dot(blocks[slot], right, preferred_element_type=jnp.float32)
                sums = product if sums is None else sums + product
        return sums

    def forward(dz):
        if dz == 0:

            def one(pp, _):
                @when((z > 0) | (pp >= p))
                def _():
                    forward_sum[...] = forward_sum[...] + forward_sums(z, pp)

                return 0

            lax.fori_loop(0, PLANE, one, 0)
        else:
            sums = forward_sum[...]
            for pp in range(PLANE):
                sums = sums + forward_sums(z + dz, pp)
            forward_sum[...] = sums

    far = list(range(planes - 1, 1, -1))

    for iteration in range(ITERS):
        last = iteration == ITERS - 1
        if iteration == 0:
            turned[...] = jnp.concatenate([start_ref[:, :size], start_ref[:, size:]], axis=0)
        gathered[me] = turned[...].T
        for h in range(2):
            for dz in far:
                when(below(dz))(lambda dz=dz, h=h: g_far(dz, h).start())
        for q in others:
            when(down_to(q))(lambda q=q: g_own(q).start())
        if planes > 1:
            when(z > 0)(lambda: g_next().start())
        g_core(0, 0).start()
        forward_sum[...] = jnp.zeros_like(forward_sum)
        if iteration == 0:
            for copy in loads:
                copy.wait()
        steps = ([("give", 1)] if planes > 1 else []) + [("give", dz) for dz in far[:1]]
        steps += [("keep", 1)] if planes > 1 else []
        for dz, after in zip(far, far[1:] + [0]):
            steps += [("give", after), ("keep", dz)]
        steps += ([] if far else [("give", 0)]) + [("keep", 0)]
        for what, dz in steps:
            when(above(dz))(lambda dz=dz, what=what: (give if what == "give" else keep)(dz))

        @when(z == 0)
        def _():
            for q in others:
                when(up_to(q))(lambda q=q: send_own(q))

        for h in range(2):
            for dz in far:

                @when(above(dz))
                def _(dz=dz, h=h):
                    g_far_in(dz, h).wait_recv()
                    for q in others:
                        g_mate(dz, q, h).start()

        for q in others:

            @when(up_to(q))
            def _(q=q):
                g_own_in(q).wait_recv()

                @when(z > 0)
                def _():
                    g_down(q).start()

                g_core(0, q).start()

        for dz in range(1, planes):

            @when(above(dz))
            def _(dz=dz):
                if dz == 1:
                    g_next_in().wait_recv()
                g_core(dz, 0).start()

        @when(z > 0)
        def _():
            for q in others:
                r_up(q).wait_recv()
                own_sum[q] = own_sum[q] + up_recv[q].astype(jnp.float32)
                send_own(q)

        for dz in far:
            for h in range(2):
                when(above(dz))(lambda dz=dz, h=h: pass_far(dz, h))

        g_core_in(0, 0).wait_recv()
        for q in others:
            when(up_to(q))(lambda q=q: g_core_in(0, q).wait_recv())
        forward(0)

        if planes > 1:

            @when(above(1))
            def _():
                for q in others:
                    g_down_in(q).wait_recv()
                    g_core(1, q).start()
                for q in range(PLANE):
                    g_core_in(1, q).wait_recv()
                forward(1)

        for dz in far:

            @when(above(dz))
            def _(dz=dz):
                for q in others:
                    for h in range(2):
                        g_mate_in(dz, q, h).wait_recv()
                    g_core(dz, q).start()

        for dz in far:

            @when(above(dz))
            def _(dz=dz):
                for q in range(PLANE):
                    g_core_in(dz, q).wait_recv()
                forward(dz)

        image[...] = forward_sum[...].T + own_sum[0]

        @when(z > 0)
        def _():
            r_up(0).wait_recv()
            image[...] = image[...] + up_recv[0].astype(jnp.float32)

        for q in others:

            @when(down_to(q))
            def _(q=q):
                r_own(q).wait_recv()
                image[...] = image[...] + mate_recv[q].astype(jnp.float32)

        for dz in range(2, planes):

            @when(below(dz))
            def _(dz=dz):
                for h in range(2):
                    r_far(dz, h).wait_recv()
                image[...] = image[...] + far_recv[dz].astype(jnp.float32)

        if planes > 1:
            when(z > 0)(lambda: g_next().wait_send())
        for dz in far:
            for h in range(2):
                when(below(dz))(lambda dz=dz, h=h: g_far(dz, h).wait_send())
        for q in others:
            when(down_to(q))(lambda q=q: g_own(q).wait_send())
            when(up_to(q))(lambda q=q: r_own(q).wait_send())
            when(up_to(q))(lambda q=q: g_core(0, q).wait_send())
            when(z > 0)(lambda q=q: g_down(q).wait_send())
        g_core(0, 0).wait_send()
        r_pair(0).wait_send()
        for dz in range(1, planes):

            @when(above(dz))
            def _(dz=dz):
                r_pair(dz).wait_send()
                for q in range(PLANE):
                    g_core(dz, q).wait_send()
                    if dz == 1:
                        r_up(q).wait_send()
                if dz >= 2:
                    for h in range(2):
                        for q in others:
                            g_mate(dz, q, h).wait_send()
                            r_mate(dz, q, h).wait_send()
                        r_far(dz, h).wait_send()

        rows = image[...]

        def diagonal_sum(square):
            return square[:columns, :columns] + square[columns:, columns:]

        gram = diagonal_sum(nt_dot(rows, rows, HIGH))
        half = columns // 2
        tall = columns if last else half
        peers = 2 * PLANE - 1
        base = iteration * 2
        rbase = iteration * (peers + planes - 1)
        sbase = iteration * (peers + 2 * planes)
        line[base, :half] = fold(gram)
        if last:
            line[base, half:] = fold(diagonal_sum(nt_dot(turned[...].astype(jnp.float32), rows, HIGH)))
        copies = []
        for i, (zz, pp, cc) in enumerate(greeted[:peers]):
            copies.append(
                remote(
                    line.at[base, pl.ds(0, tall)], line_recv.at[rbase + i, pl.ds(0, tall)],
                    ar_s.at[sbase + i], ar_r.at[sbase + i], zz, pp, cc,
                )
            )
        for copy in copies:
            copy.start()
        total = line[base, :tall]
        for i, copy in enumerate(copies):
            copy.wait()
            total = total + line_recv[rbase + i, :tall]
        line[base + 1, :tall] = total
        parts = [[], []]
        for piece in range(2 if last else 1):
            span = pl.ds(piece * half, half)
            for s in range(1, planes):
                at = sbase + peers + piece * planes + s
                copy = remote(
                    line.at[base + 1, span], line_recv.at[rbase + peers + s - 1, span],
                    ar_s.at[at], ar_r.at[at], (z + s) % planes, p, c,
                )
                copy.start()
                parts[piece].append(copy)
        for copy in parts[0]:
            copy.wait()
        summed = line[base + 1, :half]
        for s in range(1, planes):
            summed = summed + line_recv[rbase + peers + s - 1, :half]
        summed = unfold(summed / total_rows)
        inverse = inverse_factor(summed, columns)
        if last:
            inverse_ref[...] = inverse
            for copy in parts[1]:
                copy.wait()
            summed = line[base + 1, half:]
            for s in range(1, planes):
                summed = summed + line_recv[rbase + peers + s - 1, half:]
            proj_ref[...] = unfold(summed)
        for kind in range(KINDS):
            at = pl.ds(kind * columns, columns)
            if last:
                embed_ref[:, kind * size : (kind + 1) * size] = image[at]
            else:
                result = jnp.dot(
                    inverse, image[at], precision=HIGH, preferred_element_type=jnp.float32
                )
                turned[at] = result.astype(jnp.bfloat16)


def on_device(start_basis, kernel_blocks, block_row, block_col, block_count):
    devices = lax.axis_size("rows") * lax.axis_size("grp")
    me = lax.axis_index("rows") * lax.axis_size("grp") + lax.axis_index("grp")
    slots, size, _ = kernel_blocks.shape
    own_rows, columns = start_basis.shape
    per_peer = (slots + devices - 1) // devices
    planes = lax.axis_size("rows") // PLANE
    total_rows = own_rows * devices

    positions = jnp.arange(slots, dtype=jnp.int32)
    alive = positions < block_count[0]
    local_row = jnp.clip(block_row - me * KINDS, 0, KINDS - 1)
    target = block_col // KINDS
    earlier = (
        (target[:, None] == target[None, :])
        & alive[None, :]
        & (positions[None, :] < positions[:, None])
    )
    rank = jnp.sum(earlier.astype(jnp.int32), axis=1)
    spot = jnp.where(alive, target * per_peer + rank, -1)
    hit = spot[None, :] == jnp.arange(devices * per_peer, dtype=jnp.int32)[:, None]
    word = positions * 8 + local_row * 4 + (block_col - target * KINDS) * 2 + 1
    code = jnp.sum(jnp.where(hit, word[None, :], 0), axis=1)

    smem = pl.BlockSpec(memory_space=pltpu.SMEM)
    vmem = pl.BlockSpec(memory_space=pltpu.VMEM)
    dma = pltpu.SemaphoreType.DMA
    peers = 2 * PLANE - 1
    both = KINDS * columns

    def halves(*lead):
        return pltpu.VMEM((*lead, both, size), jnp.bfloat16)

    def singles(*lead):
        return pltpu.VMEM((*lead, both, size), jnp.float32)

    arounds = ITERS * (peers + 2 * planes)
    image, projected, inverse = pl.pallas_call(
        functools.partial(kernel, planes, total_rows, per_peer, columns),
        out_shape=(
            jax.ShapeDtypeStruct((columns, own_rows), jnp.float32),
            jax.ShapeDtypeStruct((columns, columns), jnp.float32),
            jax.ShapeDtypeStruct((columns, columns), jnp.float32),
        ),
        in_specs=[smem, vmem, pl.BlockSpec(memory_space=pl.ANY)],
        out_specs=(vmem, vmem, vmem),
        scratch_shapes=[
            pltpu.VMEM((slots, size, size), jnp.bfloat16),
            halves(),
            pltpu.VMEM((devices, size, both), jnp.bfloat16),
            halves(planes * PLANE),
            halves(planes * PLANE),
            halves(planes * PLANE),
            halves(planes * PLANE),
            halves(PLANE),
            halves(PLANE),
            halves(planes),
            halves(planes),
            singles(planes),
            singles(PLANE),
            pltpu.VMEM((size, both), jnp.float32),
            singles(),
            pltpu.VMEM((ITERS * 2, columns, 2 * columns), jnp.float32),
            pltpu.VMEM((ITERS * (peers + planes - 1), columns, 2 * columns), jnp.float32),
            dma((CHUNKS,)),
            dma((planes * 2,)), dma((planes * 2,)),
            dma((planes * PLANE * 2,)), dma((planes * PLANE * 2,)),
            dma((PLANE,)), dma((PLANE,)),
            dma((planes * PLANE,)), dma((planes * PLANE,)),
            dma((planes,)), dma((planes,)),
            dma((planes * PLANE * 2,)), dma((planes * PLANE * 2,)),
            dma((PLANE,)), dma((PLANE,)),
            dma((planes * 2,)), dma((planes * 2,)),
            dma((arounds,)), dma((arounds,)),
        ],
        compiler_params=pltpu.CompilerParams(
            collective_id=0, has_side_effects=True, vmem_limit_bytes=62 * 1024 * 1024
        ),
    )(code, start_basis.T, kernel_blocks)
    embedded = lax.dot_general(image, inverse, (((0,), (1,)), ((), ())), precision=HIGH)
    return embedded, projected / total_rows


def solution(mesh):
    in_specs = (
        P(("rows", "grp"), None),
        P(("rows", "grp"), None, None),
        P(("rows", "grp")),
        P(("rows", "grp")),
        P(("rows", "grp")),
    )
    out_specs = (P(("rows", "grp"), None), P())
    return jax.shard_map(
        on_device, mesh=mesh, in_specs=in_specs, out_specs=out_specs, check_vma=False
    )
```

```python
import functools

import jax
import jax.numpy as jnp
from jax import lax
from jax.experimental import pallas as pl
from jax.experimental.pallas import tpu as pltpu
from jax.sharding import PartitionSpec as P

ITERS = 2
PLANE = 4
KINDS = 2
MESH = pl.DeviceIdType.MESH
HIGH = lax.Precision.HIGHEST
CHUNKS = 4


def split_even(total, parts):
    edges = [total * i // parts for i in range(parts + 1)]
    return list(zip(edges[:-1], edges[1:]))


def nt_dot(a, b, precision=None):
    return lax.dot_general(
        a, b, (((1,), (1,)), ((), ())), preferred_element_type=jnp.float32, precision=precision
    )


def inverse_root(value):
    guess = lax.rsqrt(value)
    return guess * (1.5 - 0.5 * (value * guess) * guess)


def inverse_factor(gram, columns):
    tall = 8
    wide = 2 * columns
    row_id = lax.broadcasted_iota(jnp.int32, (columns, wide), 0)
    lane_id = lax.broadcasted_iota(jnp.int32, (columns, wide), 1)
    both = jnp.concatenate([gram, gram], axis=1)
    on_diagonal = (lane_id == row_id) | (lane_id == row_id + columns)
    diagonal = jnp.where(on_diagonal, both, 0.0)
    across = inverse_root(jnp.sum(diagonal, axis=0, keepdims=True))
    down = inverse_root(0.5 * jnp.sum(diagonal, axis=1, keepdims=True))
    unit = jnp.where(lane_id == row_id + columns, 1.0, 0.0).astype(jnp.float32)
    work = jnp.where(lane_id < columns, both * down * across, unit)
    tiles = [work[i : i + tall] for i in range(0, columns, tall)]

    def spread(row):
        return jnp.broadcast_to(row, (tall, wide))

    done = []
    for t in range(len(tiles)):
        k = t * tall
        cols = [
            [jnp.broadcast_to(tile[:, k + j : k + j + 1], (tall, wide)) for tile in tiles[t:]]
            for j in range(tall)
        ]
        rows = [spread(tiles[t][i : i + 1]) for i in range(tall)]
        p = [[spread(cols[j][0][i : i + 1]) for j in range(i + 1)] for i in range(tall)]
        inv = [None] * tall
        for j in range(0, tall, 2):
            det = p[j][j] * p[j + 1][j + 1] - p[j + 1][j] * p[j + 1][j]
            inv[j] = 1.0 / p[j][j]
            inv[j + 1] = p[j][j] * (1.0 / det)
            lead = p[j + 1][j] * inv[j]
            rows[j + 1] = rows[j + 1] - lead * rows[j]
            cols[j + 1] = [c1 - lead * c0 for c1, c0 in zip(cols[j + 1], cols[j])]
            p[j + 1][j + 1] = p[j + 1][j + 1] - lead * p[j + 1][j]
            for i in range(j + 2, tall):
                p[i][j + 1] = p[i][j + 1] - lead * p[i][j]
            for i in range(j + 2, tall):
                l0, l1 = p[i][j] * inv[j], p[i][j + 1] * inv[j + 1]
                rows[i] = rows[i] - l0 * rows[j] - l1 * rows[j + 1]
                cols[i] = [
                    ci - l0 * c0 - l1 * c1 for ci, c0, c1 in zip(cols[i], cols[j], cols[j + 1])
                ]
                for m in range(i, tall):
                    p[m][i] = p[m][i] - l0 * p[m][j] - l1 * p[m][j + 1]
        for i in range(tall):
            done.append((rows[i] * inverse_root(p[i][i]))[:1])
        scaled = [rows[i] * inv[i] for i in range(tall)]
        for at in range(t + 1, len(tiles)):
            for i in range(tall):
                tiles[at] = tiles[at] - cols[i][at - t] * scaled[i]
    return (jnp.concatenate(done, axis=0) * across)[:, columns:]


def fold(square):
    half = square.shape[0] // 2
    return jnp.concatenate([square[:half], square[half:]], axis=1)


def unfold(packed):
    half = packed.shape[1] // 2
    return jnp.concatenate([packed[:, :half], packed[:, half:]], axis=0)


def kernel(
    planes, total_rows, per_peer, columns,
    code, start_ref, blocks_hbm, embed_ref, proj_ref, inverse_ref,
    blocks, turned, gathered, pair_send, pair_recv, mate_send, mate_recv,
    up_send, up_recv, diag_send, diag_recv, far_send, far_recv, column, own_sum, forward_sum, image, line, line_recv,
    load_sem, ag_z_s, ag_z_r, ag_p_s, ag_p_r, ag_d_s, ag_d_r, ag_x_s, ag_x_r, ag_c_s, ag_c_r,
    rs_c_s, rs_c_r, rs_p_s, rs_p_r, rs_u_s, rs_u_r, rs_x_s, rs_x_r, rs_z_s, rs_z_r, ar_s, ar_r,
):
    size, both = gathered.shape[1:]
    slots = blocks.shape[0]
    rows_at = lax.axis_index("rows")
    c = lax.axis_index("grp")
    z = rows_at // PLANE
    p = rows_at % PLANE
    px, py = p % 2, p // 2

    def mate(q):
        x = px + (q % 2) * (1 - 2 * px)
        y = py + (q // 2) * (1 - 2 * py)
        return 2 * y + x

    mates = [mate(q) for q in range(PLANE)]
    others = (1, 2, 3)
    halves = ((3, 1, 2), (1, 2))

    def number(zz, pp, cc):
        return (zz * PLANE + pp) * 2 + cc

    def remote(src, dst, s, r, zz, pp, cc):
        return pltpu.make_async_remote_copy(
            src, dst, s, r, device_id=(zz * PLANE + pp, cc), device_id_type=MESH
        )

    loads = [
        pltpu.make_async_copy(
            blocks_hbm.at[pl.ds(lo, hi - lo)], blocks.at[pl.ds(lo, hi - lo)], load_sem.at[i]
        )
        for i, (lo, hi) in enumerate(split_even(slots, CHUNKS))
    ]
    for copy in loads:
        copy.start()
    barrier = pltpu.get_barrier_semaphore()
    greeted = [(z, mates[q], 1 - c if f else c) for q in range(PLANE) for f in (0, 1) if q or f]
    greeted += [((z + s) % planes, p, c) for s in range(1, planes)]
    for zz, pp, cc in greeted:
        pl.semaphore_signal(barrier, inc=1, device_id=(zz * PLANE + pp, cc), device_id_type=MESH)
    pl.semaphore_wait(barrier, len(greeted))

    def above(dz):
        return z + dz < planes

    def below(dz):
        return z - dz >= 0

    when = pl.when
    me = number(z, p, c)

    def whole(device):
        return gathered.at[device]

    def part(device, h):
        return gathered.at[device, pl.ds(h * (size // 2), size // 2)]

    def g_next():
        at = whole(me)
        return remote(at, at, ag_z_s.at[0], ag_z_r.at[0], z - 1, p, c)

    def g_next_in():
        at = whole(number(z + 1, p, c))
        return remote(at, at, ag_z_s.at[0], ag_z_r.at[0], z + 1, p, c)

    def g_far(dz, h):
        at, i = part(me, h), dz * 2 + h
        return remote(at, at, ag_z_s.at[i], ag_z_r.at[i], z - dz, p, c)

    def g_far_in(dz, h):
        at, i = part(number(z + dz, p, c), h), dz * 2 + h
        return remote(at, at, ag_z_s.at[i], ag_z_r.at[i], z + dz, p, c)

    def g_own(q):
        at = whole(me)
        return remote(at, at, ag_p_s.at[q], ag_p_r.at[q], z, mates[q], c)

    def g_own_in(q):
        at = whole(number(z, mates[q], c))
        return remote(at, at, ag_p_s.at[q], ag_p_r.at[q], z, mates[q], c)

    def g_mate(dz, q, h):
        at, i = part(number(z + dz, p, c), h), (dz * PLANE + q) * 2 + h
        return remote(at, at, ag_p_s.at[i], ag_p_r.at[i], z, mates[q], c)

    def g_mate_in(dz, q, h):
        at, i = part(number(z + dz, mates[q], c), h), (dz * PLANE + q) * 2 + h
        return remote(at, at, ag_p_s.at[i], ag_p_r.at[i], z, mates[q], c)

    def g_down(q):
        at = whole(number(z, mates[q], c))
        return remote(at, at, ag_d_s.at[q], ag_d_r.at[q], z - 1, p, c)

    def g_down_in(q):
        at = whole(number(z + 1, mates[q], c))
        return remote(at, at, ag_d_s.at[q], ag_d_r.at[q], z + 1, p, c)

    def g_diag(dz):
        at = part(number(z, mates[3], c), 1)
        return remote(at, at, ag_x_s.at[dz], ag_x_r.at[dz], z - dz, p, c)

    def g_diag_in(dz):
        at = part(number(z + dz, mates[3], c), 1)
        return remote(at, at, ag_x_s.at[dz], ag_x_r.at[dz], z + dz, p, c)

    def g_core(dz, q):
        at, i = whole(number(z + dz, mates[q], c)), dz * PLANE + q
        return remote(at, at, ag_c_s.at[i], ag_c_r.at[i], z, p, 1 - c)

    def g_core_in(dz, q):
        at, i = whole(number(z + dz, mates[q], 1 - c)), dz * PLANE + q
        return remote(at, at, ag_c_s.at[i], ag_c_r.at[i], z, p, 1 - c)

    def down_to(q):
        return (z > 0) | (mates[q] < p)

    def up_to(q):
        return (z > 0) | (mates[q] > p)

    def r_pair(dz):
        span = pl.ds(dz * PLANE, PLANE)
        return remote(
            pair_send.at[span], pair_recv.at[span], rs_c_s.at[dz], rs_c_r.at[dz], z, p, 1 - c
        )

    def r_own(q):
        return remote(
            mate_send.at[q], mate_recv.at[q], rs_p_s.at[q], rs_p_r.at[q], z, mates[q], c
        )

    def r_mate(dz, q, h):
        i = (dz * PLANE + q) * 2 + h
        at = (dz * PLANE + q, pl.ds(h * columns, columns))
        return remote(
            mate_send.at[at], mate_recv.at[at], rs_p_s.at[i], rs_p_r.at[i], z, mates[q], c
        )

    def r_up(q):
        return remote(up_send.at[q], up_recv.at[q], rs_u_s.at[q], rs_u_r.at[q], z + 1, p, c)

    def r_diag(dz):
        return remote(
            diag_send.at[dz], diag_recv.at[dz], rs_x_s.at[dz], rs_x_r.at[dz], z + dz, p, c
        )

    def r_far(dz, h):
        i = dz * 2 + h
        at = (dz, pl.ds(h * columns, columns))
        return remote(far_send.at[at], far_recv.at[at], rs_z_s.at[i], rs_z_r.at[i], z + dz, p, c)

    def decode(word):
        return word // 8, (word // 4) % 2, (word // 2) % 2, word % 2

    nothing = jnp.zeros((columns, size), jnp.bfloat16)

    def mirror_sums(device):
        sums = None
        for j in range(per_peer):
            slot, row, col, live = decode(code[device * per_peer + j])
            rows = lax.select(row == 1, turned[columns:], turned[:columns])
            left = jnp.concatenate(
                [
                    lax.select(live * (1 - col) == 1, rows, nothing),
                    lax.select(live * col == 1, rows, nothing),
                ],
                axis=0,
            )
            product = jnp.dot(left, blocks[slot], preferred_element_type=jnp.float32)
            sums = product if sums is None else sums + product
        return sums

    def give(dz):
        for pp in range(PLANE):
            pair_send[dz * PLANE + pp] = mirror_sums(number(z + dz, pp, 1 - c)).astype(
                jnp.bfloat16
            )
        r_pair(dz).start()

    def keep(dz):
        r_pair(dz).wait_recv()
        for q in others + (0,):
            pp = mates[q]
            value = mirror_sums(number(z + dz, pp, c)) + pair_recv[dz * PLANE + pp].astype(
                jnp.float32
            )
            if dz == 0:
                own_sum[q] = value
            elif dz == 1:
                up_send[q] = value.astype(jnp.bfloat16)
                r_up(q).start()
            elif q == 0:
                column[dz] = value
            elif q == 3:
                mate_send[dz * PLANE + q, :columns] = value[:columns].astype(jnp.bfloat16)
                diag_send[dz] = value[columns:].astype(jnp.bfloat16)
            else:
                mate_send[dz * PLANE + q] = value.astype(jnp.bfloat16)
        if dz >= 2:
            for h in range(2):
                for q in halves[h]:
                    r_mate(dz, q, h).start()
            r_diag(dz).start()

    def send_own(q):
        mate_send[q] = own_sum[q].astype(jnp.bfloat16)
        r_own(q).start()

    def pass_far(dz, h):
        at = pl.ds(h * columns, columns)
        total = column[dz, at]
        for q in halves[h]:
            r_mate(dz, q, h).wait_recv()
            total = total + mate_recv[dz * PLANE + q, at].astype(jnp.float32)
        far_send[dz, at] = total.astype(jnp.bfloat16)
        r_far(dz, h).start()

    lane = lax.broadcasted_iota(jnp.int32, (size, both), 1)
    sides = [
        jnp.where((lane >= columns) == bool(kind), 1.0, 0.0).astype(jnp.bfloat16)
        for kind in range(KINDS)
    ]
    neither = jnp.zeros((size, both), jnp.bfloat16)

    def forward_sums(zz, pp):
        sums = None
        for cc in range(2):
            device = number(zz, pp, cc)
            straight = gathered[device]
            crossed = jnp.concatenate([straight[:, columns:], straight[:, :columns]], axis=1)
            for j in range(per_peer):
                slot, row, col, live = decode(code[device * per_peer + j])
                side = lax.select(
                    live * (1 - row) == 1,
                    sides[0],
                    lax.select(live * row == 1, sides[1], neither),
                )
                right = lax.select(row == col, straight, crossed) * side
                product = jnp.dot(blocks[slot], right, preferred_element_type=jnp.float32)
                sums = product if sums is None else sums + product
        return sums

    def forward(dz):
        if dz == 0:

            def one(pp, _):
                @when((z > 0) | (pp >= p))
                def _():
                    forward_sum[...] = forward_sum[...] + forward_sums(z, pp)

                return 0

            lax.fori_loop(0, PLANE, one, 0)
        else:
            sums = forward_sum[...]
            for pp in range(PLANE):
                sums = sums + forward_sums(z + dz, pp)
            forward_sum[...] = sums

    far = list(range(planes - 1, 1, -1))

    for iteration in range(ITERS):
        last = iteration == ITERS - 1
        if iteration == 0:
            turned[...] = jnp.concatenate([start_ref[:, :size], start_ref[:, size:]], axis=0)
        gathered[me] = turned[...].T
        for h in range(2):
            for dz in far:
                when(below(dz))(lambda dz=dz, h=h: g_far(dz, h).start())
        for q in others:
            when(down_to(q))(lambda q=q: g_own(q).start())
        if planes > 1:
            when(z > 0)(lambda: g_next().start())
        g_core(0, 0).start()
        forward_sum[...] = jnp.zeros_like(forward_sum)
        if iteration == 0:
            for copy in loads:
                copy.wait()
        steps = ([("give", 1)] if planes > 1 else []) + [("give", dz) for dz in far[:1]]
        steps += [("keep", 1)] if planes > 1 else []
        for dz, after in zip(far, far[1:] + [0]):
            steps += [("give", after), ("keep", dz)]
        steps += ([] if far else [("give", 0)]) + [("keep", 0)]
        for what, dz in steps:
            when(above(dz))(lambda dz=dz, what=what: (give if what == "give" else keep)(dz))

        @when(z == 0)
        def _():
            for q in others:
                when(up_to(q))(lambda q=q: send_own(q))

        for h in range(2):
            for dz in far:

                @when(above(dz))
                def _(dz=dz, h=h):
                    g_far_in(dz, h).wait_recv()
                    for q in halves[h]:
                        g_mate(dz, q, h).start()

        for q in others:

            @when(up_to(q))
            def _(q=q):
                g_own_in(q).wait_recv()

                @when(z > 0)
                def _():
                    g_down(q).start()

                if q == 3:
                    for dz in far:
                        when(below(dz))(lambda dz=dz: g_diag(dz).start())

                g_core(0, q).start()

        for dz in range(1, planes):

            @when(above(dz))
            def _(dz=dz):
                if dz == 1:
                    g_next_in().wait_recv()
                g_core(dz, 0).start()

        @when(z > 0)
        def _():
            for q in others:
                r_up(q).wait_recv()
                own_sum[q] = own_sum[q] + up_recv[q].astype(jnp.float32)
                if q == 3:
                    for dz in far:

                        @when(below(dz))
                        def _(dz=dz):
                            r_diag(dz).wait_recv()
                            at = (q, pl.ds(columns, columns))
                            own_sum[at] = own_sum[at] + diag_recv[dz].astype(jnp.float32)

                send_own(q)

        for dz in far:
            for h in range(2):
                when(above(dz))(lambda dz=dz, h=h: pass_far(dz, h))

        g_core_in(0, 0).wait_recv()
        for q in others:
            when(up_to(q))(lambda q=q: g_core_in(0, q).wait_recv())
        forward(0)

        if planes > 1:

            @when(above(1))
            def _():
                for q in others:
                    g_down_in(q).wait_recv()
                    g_core(1, q).start()
                for q in range(PLANE):
                    g_core_in(1, q).wait_recv()
                forward(1)

        for dz in far:

            @when(above(dz))
            def _(dz=dz):
                for q in others:
                    for h in range(2):
                        if q in halves[h]:
                            g_mate_in(dz, q, h).wait_recv()
                        else:
                            g_diag_in(dz).wait_recv()
                    g_core(dz, q).start()

        for dz in far:

            @when(above(dz))
            def _(dz=dz):
                for q in range(PLANE):
                    g_core_in(dz, q).wait_recv()
                forward(dz)

        image[...] = forward_sum[...].T + own_sum[0]

        @when(z > 0)
        def _():
            r_up(0).wait_recv()
            image[...] = image[...] + up_recv[0].astype(jnp.float32)

        for q in others:

            @when(down_to(q))
            def _(q=q):
                r_own(q).wait_recv()
                image[...] = image[...] + mate_recv[q].astype(jnp.float32)

        for dz in range(2, planes):

            @when(below(dz))
            def _(dz=dz):
                for h in range(2):
                    r_far(dz, h).wait_recv()
                image[...] = image[...] + far_recv[dz].astype(jnp.float32)

        if planes > 1:
            when(z > 0)(lambda: g_next().wait_send())
        for dz in far:
            for h in range(2):
                when(below(dz))(lambda dz=dz, h=h: g_far(dz, h).wait_send())
        for q in others:
            when(down_to(q))(lambda q=q: g_own(q).wait_send())
            when(up_to(q))(lambda q=q: r_own(q).wait_send())
            when(up_to(q))(lambda q=q: g_core(0, q).wait_send())
            when(z > 0)(lambda q=q: g_down(q).wait_send())
        for dz in far:
            when(below(dz))(lambda dz=dz: g_diag(dz).wait_send())
        g_core(0, 0).wait_send()
        r_pair(0).wait_send()
        for dz in range(1, planes):

            @when(above(dz))
            def _(dz=dz):
                r_pair(dz).wait_send()
                for q in range(PLANE):
                    g_core(dz, q).wait_send()
                    if dz == 1:
                        r_up(q).wait_send()
                if dz >= 2:
                    r_diag(dz).wait_send()
                    for h in range(2):
                        for q in halves[h]:
                            g_mate(dz, q, h).wait_send()
                            r_mate(dz, q, h).wait_send()
                        r_far(dz, h).wait_send()

        rows = image[...]

        def diagonal_sum(square):
            return square[:columns, :columns] + square[columns:, columns:]

        gram = diagonal_sum(nt_dot(rows, rows, HIGH))
        half = columns // 2
        tall = columns if last else half
        peers = 2 * PLANE - 1
        base = iteration * 2
        rbase = iteration * (peers + planes - 1)
        sbase = iteration * (peers + 2 * planes)
        line[base, :half] = fold(gram)
        if last:
            line[base, half:] = fold(diagonal_sum(nt_dot(turned[...].astype(jnp.float32), rows, HIGH)))
        copies = []
        for i, (zz, pp, cc) in enumerate(greeted[:peers]):
            copies.append(
                remote(
                    line.at[base, pl.ds(0, tall)], line_recv.at[rbase + i, pl.ds(0, tall)],
                    ar_s.at[sbase + i], ar_r.at[sbase + i], zz, pp, cc,
                )
            )
        for copy in copies:
            copy.start()
        total = line[base, :tall]
        for i, copy in enumerate(copies):
            copy.wait()
            total = total + line_recv[rbase + i, :tall]
        line[base + 1, :tall] = total
        parts = [[], []]
        for piece in range(2 if last else 1):
            span = pl.ds(piece * half, half)
            for s in range(1, planes):
                at = sbase + peers + piece * planes + s
                copy = remote(
                    line.at[base + 1, span], line_recv.at[rbase + peers + s - 1, span],
                    ar_s.at[at], ar_r.at[at], (z + s) % planes, p, c,
                )
                copy.start()
                parts[piece].append(copy)
        for copy in parts[0]:
            copy.wait()
        summed = line[base + 1, :half]
        for s in range(1, planes):
            summed = summed + line_recv[rbase + peers + s - 1, :half]
        summed = unfold(summed / total_rows)
        inverse = inverse_factor(summed, columns)
        if last:
            inverse_ref[...] = inverse
            for copy in parts[1]:
                copy.wait()
            summed = line[base + 1, half:]
            for s in range(1, planes):
                summed = summed + line_recv[rbase + peers + s - 1, half:]
            proj_ref[...] = unfold(summed)
        for kind in range(KINDS):
            at = pl.ds(kind * columns, columns)
            if last:
                embed_ref[:, kind * size : (kind + 1) * size] = image[at]
            else:
                result = jnp.dot(
                    inverse, image[at], precision=HIGH, preferred_element_type=jnp.float32
                )
                turned[at] = result.astype(jnp.bfloat16)


def closing(total_rows, image_ref, inverse_ref, sum_ref, embed_ref, proj_ref):
    embed_ref[...] = jnp.dot(
        inverse_ref[...], image_ref[...], precision=HIGH, preferred_element_type=jnp.float32
    )
    proj_ref[...] = sum_ref[...] / total_rows


def on_device(start_basis, kernel_blocks, block_row, block_col, block_count):
    devices = lax.axis_size("rows") * lax.axis_size("grp")
    me = lax.axis_index("rows") * lax.axis_size("grp") + lax.axis_index("grp")
    slots, size, _ = kernel_blocks.shape
    own_rows, columns = start_basis.shape
    per_peer = (slots + devices - 1) // devices
    planes = lax.axis_size("rows") // PLANE
    total_rows = own_rows * devices

    positions = jnp.arange(slots, dtype=jnp.int32)
    alive = positions < block_count[0]
    local_row = jnp.clip(block_row - me * KINDS, 0, KINDS - 1)
    target = block_col // KINDS
    earlier = (
        (target[:, None] == target[None, :])
        & alive[None, :]
        & (positions[None, :] < positions[:, None])
    )
    rank = jnp.sum(earlier.astype(jnp.int32), axis=1)
    spot = jnp.where(alive, target * per_peer + rank, -1)
    hit = spot[None, :] == jnp.arange(devices * per_peer, dtype=jnp.int32)[:, None]
    word = positions * 8 + local_row * 4 + (block_col - target * KINDS) * 2 + 1
    code = jnp.sum(jnp.where(hit, word[None, :], 0), axis=1)

    smem = pl.BlockSpec(memory_space=pltpu.SMEM)
    vmem = pl.BlockSpec(memory_space=pltpu.VMEM)
    dma = pltpu.SemaphoreType.DMA
    peers = 2 * PLANE - 1
    both = KINDS * columns

    def halves(*lead):
        return pltpu.VMEM((*lead, both, size), jnp.bfloat16)

    def singles(*lead):
        return pltpu.VMEM((*lead, both, size), jnp.float32)

    arounds = ITERS * (peers + 2 * planes)
    image, projected, inverse = pl.pallas_call(
        functools.partial(kernel, planes, total_rows, per_peer, columns),
        out_shape=(
            jax.ShapeDtypeStruct((columns, own_rows), jnp.float32),
            jax.ShapeDtypeStruct((columns, columns), jnp.float32),
            jax.ShapeDtypeStruct((columns, columns), jnp.float32),
        ),
        in_specs=[smem, vmem, pl.BlockSpec(memory_space=pl.ANY)],
        out_specs=(vmem, vmem, vmem),
        scratch_shapes=[
            pltpu.VMEM((slots, size, size), jnp.bfloat16),
            halves(),
            pltpu.VMEM((devices, size, both), jnp.bfloat16),
            halves(planes * PLANE),
            halves(planes * PLANE),
            halves(planes * PLANE),
            halves(planes * PLANE),
            halves(PLANE),
            halves(PLANE),
            pltpu.VMEM((planes, columns, size), jnp.bfloat16),
            pltpu.VMEM((planes, columns, size), jnp.bfloat16),
            halves(planes),
            halves(planes),
            singles(planes),
            singles(PLANE),
            pltpu.VMEM((size, both), jnp.float32),
            singles(),
            pltpu.VMEM((ITERS * 2, columns, 2 * columns), jnp.float32),
            pltpu.VMEM((ITERS * (peers + planes - 1), columns, 2 * columns), jnp.float32),
            dma((CHUNKS,)),
            dma((planes * 2,)), dma((planes * 2,)),
            dma((planes * PLANE * 2,)), dma((planes * PLANE * 2,)),
            dma((PLANE,)), dma((PLANE,)),
            dma((planes,)), dma((planes,)),
            dma((planes * PLANE,)), dma((planes * PLANE,)),
            dma((planes,)), dma((planes,)),
            dma((planes * PLANE * 2,)), dma((planes * PLANE * 2,)),
            dma((PLANE,)), dma((PLANE,)),
            dma((planes,)), dma((planes,)),
            dma((planes * 2,)), dma((planes * 2,)),
            dma((arounds,)), dma((arounds,)),
        ],
        compiler_params=pltpu.CompilerParams(
            collective_id=0, has_side_effects=True, vmem_limit_bytes=62 * 1024 * 1024
        ),
    )(code, start_basis.T, kernel_blocks)
    embedded, projected = pl.pallas_call(
        functools.partial(closing, total_rows),
        out_shape=(
            jax.ShapeDtypeStruct((columns, own_rows), jnp.float32),
            jax.ShapeDtypeStruct((columns, columns), jnp.float32),
        ),
        in_specs=[vmem] * 3,
        out_specs=(vmem, vmem),
    )(image, inverse, projected)
    return embedded.T, projected


def solution(mesh):
    in_specs = (
        P(("rows", "grp"), None),
        P(("rows", "grp"), None, None),
        P(("rows", "grp")),
        P(("rows", "grp")),
        P(("rows", "grp")),
    )
    out_specs = (P(("rows", "grp"), None), P())
    return jax.shard_map(
        on_device, mesh=mesh, in_specs=in_specs, out_specs=out_specs, check_vma=False
    )
```

```python
import functools

import jax
import jax.numpy as jnp
from jax import lax
from jax.experimental import pallas as pl
from jax.experimental.pallas import tpu as pltpu
from jax.sharding import PartitionSpec as P

ITERS = 2
PLANE = 4
KINDS = 2
MESH = pl.DeviceIdType.MESH
HIGH = lax.Precision.HIGHEST
CHUNKS = 4


def split_even(total, parts):
    edges = [total * i // parts for i in range(parts + 1)]
    return list(zip(edges[:-1], edges[1:]))


def nt_dot(a, b, precision=None):
    return lax.dot_general(
        a, b, (((1,), (1,)), ((), ())), preferred_element_type=jnp.float32, precision=precision
    )


def inverse_root(value):
    guess = lax.rsqrt(value)
    return guess * (1.5 - 0.5 * (value * guess) * guess)


def inverse_factor(gram, columns):
    tall = 8
    wide = 2 * columns
    row_id = lax.broadcasted_iota(jnp.int32, (columns, wide), 0)
    lane_id = lax.broadcasted_iota(jnp.int32, (columns, wide), 1)
    both = jnp.concatenate([gram, gram], axis=1)
    on_diagonal = (lane_id == row_id) | (lane_id == row_id + columns)
    diagonal = jnp.where(on_diagonal, both, 0.0)
    across = inverse_root(jnp.sum(diagonal, axis=0, keepdims=True))
    down = inverse_root(0.5 * jnp.sum(diagonal, axis=1, keepdims=True))
    unit = jnp.where(lane_id == row_id + columns, 1.0, 0.0).astype(jnp.float32)
    work = jnp.where(lane_id < columns, both * down * across, unit)
    tiles = [work[i : i + tall] for i in range(0, columns, tall)]

    def spread(row):
        return jnp.broadcast_to(row, (tall, wide))

    done = []
    for t in range(len(tiles)):
        k = t * tall
        cols = [
            [jnp.broadcast_to(tile[:, k + j : k + j + 1], (tall, wide)) for tile in tiles[t:]]
            for j in range(tall)
        ]
        rows = [spread(tiles[t][i : i + 1]) for i in range(tall)]
        p = [[spread(cols[j][0][i : i + 1]) for j in range(i + 1)] for i in range(tall)]
        inv = [None] * tall
        for j in range(0, tall, 2):
            det = p[j][j] * p[j + 1][j + 1] - p[j + 1][j] * p[j + 1][j]
            inv[j] = 1.0 / p[j][j]
            inv[j + 1] = p[j][j] * (1.0 / det)
            lead = p[j + 1][j] * inv[j]
            rows[j + 1] = rows[j + 1] - lead * rows[j]
            cols[j + 1] = [c1 - lead * c0 for c1, c0 in zip(cols[j + 1], cols[j])]
            p[j + 1][j + 1] = p[j + 1][j + 1] - lead * p[j + 1][j]
            for i in range(j + 2, tall):
                p[i][j + 1] = p[i][j + 1] - lead * p[i][j]
            for i in range(j + 2, tall):
                l0, l1 = p[i][j] * inv[j], p[i][j + 1] * inv[j + 1]
                rows[i] = rows[i] - l0 * rows[j] - l1 * rows[j + 1]
                cols[i] = [
                    ci - l0 * c0 - l1 * c1 for ci, c0, c1 in zip(cols[i], cols[j], cols[j + 1])
                ]
                for m in range(i, tall):
                    p[m][i] = p[m][i] - l0 * p[m][j] - l1 * p[m][j + 1]
        for i in range(tall):
            done.append((rows[i] * inverse_root(p[i][i]))[:1])
        scaled = [rows[i] * inv[i] for i in range(tall)]
        for at in range(t + 1, len(tiles)):
            for i in range(tall):
                tiles[at] = tiles[at] - cols[i][at - t] * scaled[i]
    return (jnp.concatenate(done, axis=0) * across)[:, columns:]


def fold(square):
    half = square.shape[0] // 2
    return jnp.concatenate([square[:half], square[half:]], axis=1)


def unfold(packed):
    half = packed.shape[1] // 2
    return jnp.concatenate([packed[:, :half], packed[:, half:]], axis=0)


def kernel(
    planes, total_rows, per_peer, columns,
    code, start_ref, blocks_hbm, embed_ref, proj_ref, inverse_ref,
    blocks, turned, gathered, pair_send, pair_recv, mate_send, mate_recv,
    up_send, up_recv, diag_send, diag_recv, far_send, far_recv, column, own_sum, forward_sum, image, line, line_recv,
    load_sem, ag_z_s, ag_z_r, ag_p_s, ag_p_r, ag_d_s, ag_d_r, ag_x_s, ag_x_r, ag_c_s, ag_c_r,
    rs_c_s, rs_c_r, rs_p_s, rs_p_r, rs_u_s, rs_u_r, rs_x_s, rs_x_r, rs_z_s, rs_z_r, ar_s, ar_r,
):
    size, both = gathered.shape[1:]
    slots = blocks.shape[0]
    rows_at = lax.axis_index("rows")
    c = lax.axis_index("grp")
    z = rows_at // PLANE
    p = rows_at % PLANE
    px, py = p % 2, p // 2

    def mate(q):
        x = px + (q % 2) * (1 - 2 * px)
        y = py + (q // 2) * (1 - 2 * py)
        return 2 * y + x

    mates = [mate(q) for q in range(PLANE)]
    others = (1, 2, 3)
    halves = ((3, 1, 2), (1, 2))

    def number(zz, pp, cc):
        return (zz * PLANE + pp) * 2 + cc

    def remote(src, dst, s, r, zz, pp, cc):
        return pltpu.make_async_remote_copy(
            src, dst, s, r, device_id=(zz * PLANE + pp, cc), device_id_type=MESH
        )

    loads = [
        pltpu.make_async_copy(
            blocks_hbm.at[pl.ds(lo, hi - lo)], blocks.at[pl.ds(lo, hi - lo)], load_sem.at[i]
        )
        for i, (lo, hi) in enumerate(split_even(slots, CHUNKS))
    ]
    for copy in loads:
        copy.start()
    barrier = pltpu.get_barrier_semaphore()
    greeted = [(z, mates[q], 1 - c if f else c) for q in range(PLANE) for f in (0, 1) if q or f]
    greeted += [((z + s) % planes, p, c) for s in range(1, planes)]
    for zz, pp, cc in greeted:
        pl.semaphore_signal(barrier, inc=1, device_id=(zz * PLANE + pp, cc), device_id_type=MESH)
    pl.semaphore_wait(barrier, len(greeted))

    def above(dz):
        return z + dz < planes

    def below(dz):
        return z - dz >= 0

    when = pl.when
    me = number(z, p, c)

    def whole(device):
        return gathered.at[device]

    def part(device, h):
        return gathered.at[device, pl.ds(h * (size // 2), size // 2)]

    def g_next():
        at = whole(me)
        return remote(at, at, ag_z_s.at[0], ag_z_r.at[0], z - 1, p, c)

    def g_next_in():
        at = whole(number(z + 1, p, c))
        return remote(at, at, ag_z_s.at[0], ag_z_r.at[0], z + 1, p, c)

    def g_far(dz, h):
        at, i = part(me, h), dz * 2 + h
        return remote(at, at, ag_z_s.at[i], ag_z_r.at[i], z - dz, p, c)

    def g_far_in(dz, h):
        at, i = part(number(z + dz, p, c), h), dz * 2 + h
        return remote(at, at, ag_z_s.at[i], ag_z_r.at[i], z + dz, p, c)

    def g_own(q):
        at = whole(me)
        return remote(at, at, ag_p_s.at[q], ag_p_r.at[q], z, mates[q], c)

    def g_own_in(q):
        at = whole(number(z, mates[q], c))
        return remote(at, at, ag_p_s.at[q], ag_p_r.at[q], z, mates[q], c)

    def g_mate(dz, q, h):
        at, i = part(number(z + dz, p, c), h), (dz * PLANE + q) * 2 + h
        return remote(at, at, ag_p_s.at[i], ag_p_r.at[i], z, mates[q], c)

    def g_mate_in(dz, q, h):
        at, i = part(number(z + dz, mates[q], c), h), (dz * PLANE + q) * 2 + h
        return remote(at, at, ag_p_s.at[i], ag_p_r.at[i], z, mates[q], c)

    def g_down(q):
        at = whole(number(z, mates[q], c))
        return remote(at, at, ag_d_s.at[q], ag_d_r.at[q], z - 1, p, c)

    def g_down_in(q):
        at = whole(number(z + 1, mates[q], c))
        return remote(at, at, ag_d_s.at[q], ag_d_r.at[q], z + 1, p, c)

    def g_diag(dz):
        at = part(number(z, mates[3], c), 1)
        return remote(at, at, ag_x_s.at[dz], ag_x_r.at[dz], z - dz, p, c)

    def g_diag_in(dz):
        at = part(number(z + dz, mates[3], c), 1)
        return remote(at, at, ag_x_s.at[dz], ag_x_r.at[dz], z + dz, p, c)

    def g_core(dz, q):
        at, i = whole(number(z + dz, mates[q], c)), dz * PLANE + q
        return remote(at, at, ag_c_s.at[i], ag_c_r.at[i], z, p, 1 - c)

    def g_core_in(dz, q):
        at, i = whole(number(z + dz, mates[q], 1 - c)), dz * PLANE + q
        return remote(at, at, ag_c_s.at[i], ag_c_r.at[i], z, p, 1 - c)

    def down_to(q):
        return (z > 0) | (mates[q] < p)

    def up_to(q):
        return (z > 0) | (mates[q] > p)

    def r_pair(dz):
        span = pl.ds(dz * PLANE, PLANE)
        return remote(
            pair_send.at[span], pair_recv.at[span], rs_c_s.at[dz], rs_c_r.at[dz], z, p, 1 - c
        )

    def r_own(q, h):
        i, at = q * 2 + h, (q, pl.ds(h * columns, columns))
        return remote(
            mate_send.at[at], mate_recv.at[at], rs_p_s.at[i], rs_p_r.at[i], z, mates[q], c
        )

    def r_mate(dz, q, h):
        i = (dz * PLANE + q) * 2 + h
        at = (dz * PLANE + q, pl.ds(h * columns, columns))
        return remote(
            mate_send.at[at], mate_recv.at[at], rs_p_s.at[i], rs_p_r.at[i], z, mates[q], c
        )

    def r_up(q):
        return remote(up_send.at[q], up_recv.at[q], rs_u_s.at[q], rs_u_r.at[q], z + 1, p, c)

    def r_diag(dz):
        return remote(
            diag_send.at[dz], diag_recv.at[dz], rs_x_s.at[dz], rs_x_r.at[dz], z + dz, p, c
        )

    def r_far(dz, h):
        i = dz * 2 + h
        at = (dz, pl.ds(h * columns, columns))
        return remote(far_send.at[at], far_recv.at[at], rs_z_s.at[i], rs_z_r.at[i], z + dz, p, c)

    def decode(word):
        return word // 8, (word // 4) % 2, (word // 2) % 2, word % 2

    nothing = jnp.zeros((columns, size), jnp.bfloat16)

    def mirror_sums(device):
        sums = None
        for j in range(per_peer):
            slot, row, col, live = decode(code[device * per_peer + j])
            rows = lax.select(row == 1, turned[columns:], turned[:columns])
            left = jnp.concatenate(
                [
                    lax.select(live * (1 - col) == 1, rows, nothing),
                    lax.select(live * col == 1, rows, nothing),
                ],
                axis=0,
            )
            product = jnp.dot(left, blocks[slot], preferred_element_type=jnp.float32)
            sums = product if sums is None else sums + product
        return sums

    def give(dz):
        for pp in range(PLANE):
            pair_send[dz * PLANE + pp] = mirror_sums(number(z + dz, pp, 1 - c)).astype(
                jnp.bfloat16
            )
        r_pair(dz).start()

    def keep(dz):
        r_pair(dz).wait_recv()
        for q in others + (0,):
            pp = mates[q]
            value = mirror_sums(number(z + dz, pp, c)) + pair_recv[dz * PLANE + pp].astype(
                jnp.float32
            )
            if dz == 0:
                own_sum[q] = value
            elif dz == 1:
                up_send[q] = value.astype(jnp.bfloat16)
                if q:
                    r_up(q).start()
            elif q == 0:
                column[dz] = value
            elif q == 3:
                mate_send[dz * PLANE + q, :columns] = value[:columns].astype(jnp.bfloat16)
                diag_send[dz] = value[columns:].astype(jnp.bfloat16)
            else:
                mate_send[dz * PLANE + q] = value.astype(jnp.bfloat16)
        if dz >= 2:
            for h in range(2):
                for q in halves[h]:
                    r_mate(dz, q, h).start()
            r_diag(dz).start()

    def send_own(q, h):
        at = (q, pl.ds(h * columns, columns))
        mate_send[at] = own_sum[at].astype(jnp.bfloat16)
        r_own(q, h).start()

    def pass_far(dz, h):
        at = pl.ds(h * columns, columns)
        total = column[dz, at]
        for q in halves[h]:
            r_mate(dz, q, h).wait_recv()
            total = total + mate_recv[dz * PLANE + q, at].astype(jnp.float32)
        far_send[dz, at] = total.astype(jnp.bfloat16)
        r_far(dz, h).start()

    lane = lax.broadcasted_iota(jnp.int32, (size, both), 1)
    sides = [
        jnp.where((lane >= columns) == bool(kind), 1.0, 0.0).astype(jnp.bfloat16)
        for kind in range(KINDS)
    ]
    neither = jnp.zeros((size, both), jnp.bfloat16)

    def forward_sums(zz, pp, lanes):
        sums = None
        for cc in lanes:
            device = number(zz, pp, cc)
            straight = gathered[device]
            crossed = jnp.concatenate([straight[:, columns:], straight[:, :columns]], axis=1)
            for j in range(per_peer):
                slot, row, col, live = decode(code[device * per_peer + j])
                side = lax.select(
                    live * (1 - row) == 1,
                    sides[0],
                    lax.select(live * row == 1, sides[1], neither),
                )
                right = lax.select(row == col, straight, crossed) * side
                product = jnp.dot(blocks[slot], right, preferred_element_type=jnp.float32)
                sums = product if sums is None else sums + product
        return sums

    def forward(dz, lane_at=None):
        if dz == 0:

            def one(pp, _):
                @when((z > 0) | (pp >= p))
                def _():
                    forward_sum[...] = forward_sum[...] + forward_sums(z, pp, (0, 1))

                return 0

            lax.fori_loop(0, PLANE, one, 0)
        else:
            sums = forward_sum[...]
            for pp in range(PLANE):
                sums = sums + forward_sums(z + dz, pp, (lane_at,))
            forward_sum[...] = sums

    far = list(range(planes - 1, 1, -1))

    for iteration in range(ITERS):
        last = iteration == ITERS - 1
        if iteration == 0:
            turned[...] = jnp.concatenate([start_ref[:, :size], start_ref[:, size:]], axis=0)
        gathered[me] = turned[...].T
        for h in range(2):
            for dz in far:
                when(below(dz))(lambda dz=dz, h=h: g_far(dz, h).start())
        for q in others:
            when(down_to(q))(lambda q=q: g_own(q).start())
        g_core(0, 0).start()
        forward_sum[...] = jnp.zeros_like(forward_sum)
        if iteration == 0:
            for copy in loads:
                copy.wait()
        steps = ([("give", 1)] if planes > 1 else []) + [("give", dz) for dz in far[:1]]
        steps += [("keep", 1)] if planes > 1 else []
        for dz, after in zip(far, far[1:] + [0]):
            steps += [("give", after), ("keep", dz)]
        steps += ([] if far else [("give", 0)]) + [("keep", 0)]
        for what, dz in steps:
            when(above(dz))(lambda dz=dz, what=what: (give if what == "give" else keep)(dz))
            if (what, dz) == ("keep", 1):
                when(z > 0)(lambda: g_next().start())
        if planes > 1:
            when(above(1))(lambda: r_up(0).start())

        @when(z == 0)
        def _():
            for q in others:
                for h in range(2):
                    when(up_to(q))(lambda q=q, h=h: send_own(q, h))

        for h in range(2):
            for dz in far:

                @when(above(dz))
                def _(dz=dz, h=h):
                    g_far_in(dz, h).wait_recv()
                    for q in halves[h]:
                        g_mate(dz, q, h).start()
                    if h == 1:
                        g_core(dz, 0).start()

        for q in others:

            @when(up_to(q))
            def _(q=q):
                g_own_in(q).wait_recv()

                @when(z > 0)
                def _():
                    g_down(q).start()

                if q == 3:
                    for dz in far:
                        when(below(dz))(lambda dz=dz: g_diag(dz).start())

                g_core(0, q).start()

        @when(z > 0)
        def _():
            for q in others:
                r_up(q).wait_recv()
                own_sum[q] = own_sum[q] + up_recv[q].astype(jnp.float32)
                send_own(q, 0)
                if q == 3:
                    for dz in far:

                        @when(below(dz))
                        def _(dz=dz):
                            r_diag(dz).wait_recv()
                            at = (q, pl.ds(columns, columns))
                            own_sum[at] = own_sum[at] + diag_recv[dz].astype(jnp.float32)

                send_own(q, 1)

        for dz in far:
            for h in range(2):
                when(above(dz))(lambda dz=dz, h=h: pass_far(dz, h))

        g_core_in(0, 0).wait_recv()
        for q in others:
            when(up_to(q))(lambda q=q: g_core_in(0, q).wait_recv())
        forward(0)

        if planes > 1:

            @when(above(1))
            def _():
                g_next_in().wait_recv()
                g_core(1, 0).start()
                for q in others:
                    g_down_in(q).wait_recv()
                    g_core(1, q).start()
                forward(1, c)
                for q in range(PLANE):
                    g_core_in(1, q).wait_recv()
                forward(1, 1 - c)

        def other_lane(dz):
            for q in range(PLANE):
                g_core_in(dz, q).wait_recv()
            forward(dz, 1 - c)

        for dz in far:

            @when(above(dz))
            def _(dz=dz):
                for q in others:
                    for h in range(2):
                        if q in halves[h]:
                            g_mate_in(dz, q, h).wait_recv()
                        else:
                            g_diag_in(dz).wait_recv()
                    g_core(dz, q).start()
                forward(dz, c)
                if dz < planes - 1:
                    when(above(dz + 1))(lambda: other_lane(dz + 1))

        if far:
            when(above(2))(lambda: other_lane(2))

        if planes > 1:
            when(z > 0)(lambda: g_next().wait_send())
        for dz in far:

            @when(below(dz))
            def _(dz=dz):
                for h in range(2):
                    g_far(dz, h).wait_send()
                g_diag(dz).wait_send()

        g_core(0, 0).wait_send()
        for q in others:
            when(down_to(q))(lambda q=q: g_own(q).wait_send())
            when(up_to(q))(lambda q=q: g_core(0, q).wait_send())
            when(z > 0)(lambda q=q: g_down(q).wait_send())
        for dz in range(1, planes):

            @when(above(dz))
            def _(dz=dz):
                for q in range(PLANE):
                    g_core(dz, q).wait_send()
                if dz >= 2:
                    for h in range(2):
                        for q in halves[h]:
                            g_mate(dz, q, h).wait_send()

        image[...] = forward_sum[...].T + own_sum[0]

        @when(z > 0)
        def _():
            r_up(0).wait_recv()
            image[...] = image[...] + up_recv[0].astype(jnp.float32)

        for q in others:

            @when(down_to(q))
            def _(q=q):
                for h in range(2):
                    r_own(q, h).wait_recv()
                image[...] = image[...] + mate_recv[q].astype(jnp.float32)

        for dz in range(2, planes):

            @when(below(dz))
            def _(dz=dz):
                for h in range(2):
                    r_far(dz, h).wait_recv()
                image[...] = image[...] + far_recv[dz].astype(jnp.float32)

        rows = image[...]

        def diagonal_sum(square):
            return square[:columns, :columns] + square[columns:, columns:]

        gram = diagonal_sum(nt_dot(rows, rows, HIGH))
        half = columns // 2
        tall = columns if last else half
        peers = 2 * PLANE - 1
        base = iteration * 2
        rbase = iteration * (peers + planes - 1)
        sbase = iteration * (peers + 2 * planes)
        line[base, :half] = fold(gram)
        if last:
            line[base, half:] = fold(diagonal_sum(nt_dot(turned[...].astype(jnp.float32), rows, HIGH)))
        copies = []
        for i, (zz, pp, cc) in enumerate(greeted[:peers]):
            copies.append(
                remote(
                    line.at[base, pl.ds(0, tall)], line_recv.at[rbase + i, pl.ds(0, tall)],
                    ar_s.at[sbase + i], ar_r.at[sbase + i], zz, pp, cc,
                )
            )
        for copy in copies:
            copy.start()
        for q in others:
            for h in range(2):
                when(up_to(q))(lambda q=q, h=h: r_own(q, h).wait_send())
        r_pair(0).wait_send()
        for dz in range(1, planes):

            @when(above(dz))
            def _(dz=dz):
                r_pair(dz).wait_send()
                if dz == 1:
                    for q in range(PLANE):
                        r_up(q).wait_send()
                else:
                    r_diag(dz).wait_send()
                    for h in range(2):
                        for q in halves[h]:
                            r_mate(dz, q, h).wait_send()
                        r_far(dz, h).wait_send()

        total = line[base, :tall]
        for i, copy in enumerate(copies):
            copy.wait()
            total = total + line_recv[rbase + i, :tall]
        line[base + 1, :tall] = total
        parts = [[], []]
        for piece in range(2 if last else 1):
            span = pl.ds(piece * half, half)
            for s in range(1, planes):
                at = sbase + peers + piece * planes + s
                copy = remote(
                    line.at[base + 1, span], line_recv.at[rbase + peers + s - 1, span],
                    ar_s.at[at], ar_r.at[at], (z + s) % planes, p, c,
                )
                copy.start()
                parts[piece].append(copy)
        for copy in parts[0]:
            copy.wait()
        summed = line[base + 1, :half]
        for s in range(1, planes):
            summed = summed + line_recv[rbase + peers + s - 1, :half]
        summed = unfold(summed / total_rows)
        inverse = inverse_factor(summed, columns)
        if last:
            inverse_ref[...] = inverse
            for copy in parts[1]:
                copy.wait()
            summed = line[base + 1, half:]
            for s in range(1, planes):
                summed = summed + line_recv[rbase + peers + s - 1, half:]
            proj_ref[...] = unfold(summed)
        for kind in range(KINDS):
            at = pl.ds(kind * columns, columns)
            if last:
                embed_ref[:, kind * size : (kind + 1) * size] = image[at]
            else:
                result = jnp.dot(
                    inverse, image[at], precision=HIGH, preferred_element_type=jnp.float32
                )
                turned[at] = result.astype(jnp.bfloat16)


def closing(total_rows, image_ref, inverse_ref, sum_ref, embed_ref, proj_ref):
    embed_ref[...] = jnp.dot(
        inverse_ref[...], image_ref[...], precision=HIGH, preferred_element_type=jnp.float32
    )
    proj_ref[...] = sum_ref[...] / total_rows


def on_device(start_basis, kernel_blocks, block_row, block_col, block_count):
    devices = lax.axis_size("rows") * lax.axis_size("grp")
    me = lax.axis_index("rows") * lax.axis_size("grp") + lax.axis_index("grp")
    slots, size, _ = kernel_blocks.shape
    own_rows, columns = start_basis.shape
    per_peer = (slots + devices - 1) // devices
    planes = lax.axis_size("rows") // PLANE
    total_rows = own_rows * devices

    positions = jnp.arange(slots, dtype=jnp.int32)
    alive = positions < block_count[0]
    local_row = jnp.clip(block_row - me * KINDS, 0, KINDS - 1)
    target = block_col // KINDS
    earlier = (
        (target[:, None] == target[None, :])
        & alive[None, :]
        & (positions[None, :] < positions[:, None])
    )
    rank = jnp.sum(earlier.astype(jnp.int32), axis=1)
    spot = jnp.where(alive, target * per_peer + rank, -1)
    hit = spot[None, :] == jnp.arange(devices * per_peer, dtype=jnp.int32)[:, None]
    word = positions * 8 + local_row * 4 + (block_col - target * KINDS) * 2 + 1
    code = jnp.sum(jnp.where(hit, word[None, :], 0), axis=1)

    smem = pl.BlockSpec(memory_space=pltpu.SMEM)
    vmem = pl.BlockSpec(memory_space=pltpu.VMEM)
    dma = pltpu.SemaphoreType.DMA
    peers = 2 * PLANE - 1
    both = KINDS * columns

    def halves(*lead):
        return pltpu.VMEM((*lead, both, size), jnp.bfloat16)

    def singles(*lead):
        return pltpu.VMEM((*lead, both, size), jnp.float32)

    arounds = ITERS * (peers + 2 * planes)
    image, projected, inverse = pl.pallas_call(
        functools.partial(kernel, planes, total_rows, per_peer, columns),
        out_shape=(
            jax.ShapeDtypeStruct((columns, own_rows), jnp.float32),
            jax.ShapeDtypeStruct((columns, columns), jnp.float32),
            jax.ShapeDtypeStruct((columns, columns), jnp.float32),
        ),
        in_specs=[smem, vmem, pl.BlockSpec(memory_space=pl.ANY)],
        out_specs=(vmem, vmem, vmem),
        scratch_shapes=[
            pltpu.VMEM((slots, size, size), jnp.bfloat16),
            halves(),
            pltpu.VMEM((devices, size, both), jnp.bfloat16),
            halves(planes * PLANE),
            halves(planes * PLANE),
            halves(planes * PLANE),
            halves(planes * PLANE),
            halves(PLANE),
            halves(PLANE),
            pltpu.VMEM((planes, columns, size), jnp.bfloat16),
            pltpu.VMEM((planes, columns, size), jnp.bfloat16),
            halves(planes),
            halves(planes),
            singles(planes),
            singles(PLANE),
            pltpu.VMEM((size, both), jnp.float32),
            singles(),
            pltpu.VMEM((ITERS * 2, columns, 2 * columns), jnp.float32),
            pltpu.VMEM((ITERS * (peers + planes - 1), columns, 2 * columns), jnp.float32),
            dma((CHUNKS,)),
            dma((planes * 2,)), dma((planes * 2,)),
            dma((planes * PLANE * 2,)), dma((planes * PLANE * 2,)),
            dma((PLANE,)), dma((PLANE,)),
            dma((planes,)), dma((planes,)),
            dma((planes * PLANE,)), dma((planes * PLANE,)),
            dma((planes,)), dma((planes,)),
            dma((planes * PLANE * 2,)), dma((planes * PLANE * 2,)),
            dma((PLANE,)), dma((PLANE,)),
            dma((planes,)), dma((planes,)),
            dma((planes * 2,)), dma((planes * 2,)),
            dma((arounds,)), dma((arounds,)),
        ],
        compiler_params=pltpu.CompilerParams(
            collective_id=0, has_side_effects=True, vmem_limit_bytes=62 * 1024 * 1024
        ),
    )(code, start_basis.T, kernel_blocks)
    embedded, projected = pl.pallas_call(
        functools.partial(closing, total_rows),
        out_shape=(
            jax.ShapeDtypeStruct((columns, own_rows), jnp.float32),
            jax.ShapeDtypeStruct((columns, columns), jnp.float32),
        ),
        in_specs=[vmem] * 3,
        out_specs=(vmem, vmem),
    )(image, inverse, projected)
    return embedded.T, projected


def solution(mesh):
    in_specs = (
        P(("rows", "grp"), None),
        P(("rows", "grp"), None, None),
        P(("rows", "grp")),
        P(("rows", "grp")),
        P(("rows", "grp")),
    )
    out_specs = (P(("rows", "grp"), None), P())
    return jax.shard_map(
        on_device, mesh=mesh, in_specs=in_specs, out_specs=out_specs, check_vma=False
    )
```

```python
import functools

import jax
import jax.numpy as jnp
from jax import lax
from jax.experimental import pallas as pl
from jax.experimental.pallas import tpu as pltpu
from jax.sharding import PartitionSpec as P

ITERS = 2
PLANE = 4
KINDS = 2
MESH = pl.DeviceIdType.MESH
HIGH = lax.Precision.HIGHEST
CHUNKS = 4


def split_even(total, parts):
    edges = [total * i // parts for i in range(parts + 1)]
    return list(zip(edges[:-1], edges[1:]))


def nt_dot(a, b, precision=None):
    return lax.dot_general(
        a, b, (((1,), (1,)), ((), ())), preferred_element_type=jnp.float32, precision=precision
    )


def inverse_root(value):
    guess = lax.rsqrt(value)
    return guess * (1.5 - 0.5 * (value * guess) * guess)


def inverse_factor(gram, columns):
    tall = 8
    wide = 2 * columns
    row_id = lax.broadcasted_iota(jnp.int32, (columns, wide), 0)
    lane_id = lax.broadcasted_iota(jnp.int32, (columns, wide), 1)
    both = jnp.concatenate([gram, gram], axis=1)
    on_diagonal = (lane_id == row_id) | (lane_id == row_id + columns)
    diagonal = jnp.where(on_diagonal, both, 0.0)
    across = inverse_root(jnp.sum(diagonal, axis=0, keepdims=True))
    down = inverse_root(0.5 * jnp.sum(diagonal, axis=1, keepdims=True))
    unit = jnp.where(lane_id == row_id + columns, 1.0, 0.0).astype(jnp.float32)
    work = jnp.where(lane_id < columns, both * down * across, unit)
    tiles = [work[i : i + tall] for i in range(0, columns, tall)]

    def spread(row):
        return jnp.broadcast_to(row, (tall, wide))

    done = []
    for t in range(len(tiles)):
        k = t * tall
        cols = [
            [jnp.broadcast_to(tile[:, k + j : k + j + 1], (tall, wide)) for tile in tiles[t:]]
            for j in range(tall)
        ]
        rows = [spread(tiles[t][i : i + 1]) for i in range(tall)]
        p = [[spread(cols[j][0][i : i + 1]) for j in range(i + 1)] for i in range(tall)]
        inv = [None] * tall
        for j in range(0, tall, 2):
            det = p[j][j] * p[j + 1][j + 1] - p[j + 1][j] * p[j + 1][j]
            inv[j] = 1.0 / p[j][j]
            inv[j + 1] = p[j][j] * (1.0 / det)
            lead = p[j + 1][j] * inv[j]
            rows[j + 1] = rows[j + 1] - lead * rows[j]
            cols[j + 1] = [c1 - lead * c0 for c1, c0 in zip(cols[j + 1], cols[j])]
            p[j + 1][j + 1] = p[j + 1][j + 1] - lead * p[j + 1][j]
            for i in range(j + 2, tall):
                p[i][j + 1] = p[i][j + 1] - lead * p[i][j]
            for i in range(j + 2, tall):
                l0, l1 = p[i][j] * inv[j], p[i][j + 1] * inv[j + 1]
                rows[i] = rows[i] - l0 * rows[j] - l1 * rows[j + 1]
                cols[i] = [
                    ci - l0 * c0 - l1 * c1 for ci, c0, c1 in zip(cols[i], cols[j], cols[j + 1])
                ]
                for m in range(i, tall):
                    p[m][i] = p[m][i] - l0 * p[m][j] - l1 * p[m][j + 1]
        for i in range(tall):
            done.append((rows[i] * inverse_root(p[i][i]))[:1])
        scaled = [rows[i] * inv[i] for i in range(tall)]
        for at in range(t + 1, len(tiles)):
            for i in range(tall):
                tiles[at] = tiles[at] - cols[i][at - t] * scaled[i]
    return (jnp.concatenate(done, axis=0) * across)[:, columns:]


def fold(square):
    half = square.shape[0] // 2
    return jnp.concatenate([square[:half], square[half:]], axis=1)


def unfold(packed):
    half = packed.shape[1] // 2
    return jnp.concatenate([packed[:, :half], packed[:, half:]], axis=0)


def semaphores(planes):
    far, others = range(2, planes), range(1, PLANE)
    names = ["next", "next_s"]
    for iteration in range(ITERS):
        names += [(stage + side, iteration) for stage in ("plane", "gram", "proj") for side in ("", "_s")]
    names += [("own", q) for q in others] + [("own_s", q) for q in others]
    names += [("down", q) for q in others] + [("core0", q) for q in range(PLANE)]
    names += [("core0_s", q) for q in range(PLANE)] + [("up", q) for q in range(PLANE)]
    names += [("share", q) for q in others] + [("share_s", q) for q in others]
    names += [("core", dz) for dz in range(1, planes)] + [("above_s", dz) for dz in range(1, planes)]
    names += [("pair", dz) for dz in range(planes)] + [("reduce_s", dz) for dz in range(planes)]
    for dz in far:
        names += [(name, dz) for name in ("far_s", "diag", "r_diag", "r_far")]
        names += [(name, dz, h) for name in ("far", "r_mate") for h in range(2)]
        names += [("mate", dz, q, h) for h in range(2) for q in (others if h == 0 else (1, 2))]
    return {name: i for i, name in enumerate(names)}


def kernel(
    planes, total_rows, per_peer, columns,
    code, start_ref, blocks_hbm, embed_ref, proj_ref, inverse_ref,
    blocks, turned, gathered, pair_send, pair_recv, mate_send, mate_recv,
    up_send, up_recv, diag_send, diag_recv, far_send, far_recv, column, own_sum, forward_sum, image, line, line_recv,
    load_sem, sems,
):
    size, both = gathered.shape[1:]
    slots = blocks.shape[0]
    rows_at = lax.axis_index("rows")
    c = lax.axis_index("grp")
    z = rows_at // PLANE
    p = rows_at % PLANE
    px, py = p % 2, p // 2

    def mate(q):
        x = px + (q % 2) * (1 - 2 * px)
        y = py + (q // 2) * (1 - 2 * py)
        return 2 * y + x

    mates = [mate(q) for q in range(PLANE)]
    places = semaphores(planes)

    def sem(*name):
        return sems.at[places[name if len(name) > 1 else name[0]]]
    others = (1, 2, 3)
    halves = ((3, 1, 2), (1, 2))

    def number(zz, pp, cc):
        return (zz * PLANE + pp) * 2 + cc

    def remote(src, dst, s, r, zz, pp, cc):
        return pltpu.make_async_remote_copy(
            src, dst, s, r, device_id=(zz * PLANE + pp, cc), device_id_type=MESH
        )

    loads = [
        pltpu.make_async_copy(
            blocks_hbm.at[pl.ds(lo, hi - lo)], blocks.at[pl.ds(lo, hi - lo)], load_sem.at[i]
        )
        for i, (lo, hi) in enumerate(split_even(slots, CHUNKS))
    ]
    for copy in loads:
        copy.start()
    barrier = pltpu.get_barrier_semaphore()
    greeted = [(z, mates[q], 1 - c if f else c) for q in range(PLANE) for f in (0, 1) if q or f]
    greeted += [((z + s) % planes, p, c) for s in range(1, planes)]
    for zz, pp, cc in greeted:
        pl.semaphore_signal(barrier, inc=1, device_id=(zz * PLANE + pp, cc), device_id_type=MESH)
    turned[...] = jnp.concatenate([start_ref[:, :size], start_ref[:, size:]], axis=0)
    gathered[number(z, p, c)] = turned[...].T
    pl.semaphore_wait(barrier, len(greeted))

    def above(dz):
        return z + dz < planes

    def below(dz):
        return z - dz >= 0

    when = pl.when
    me = number(z, p, c)

    def whole(device):
        return gathered.at[device]

    def part(device, h):
        return gathered.at[device, pl.ds(h * (size // 2), size // 2)]

    def g_next():
        at = whole(me)
        return remote(at, at, sem("next_s"), sem("next"), z - 1, p, c)

    def g_next_in():
        at = whole(number(z + 1, p, c))
        return remote(at, at, sem("next_s"), sem("next"), z + 1, p, c)

    def g_far(dz, h):
        at = part(me, h)
        return remote(at, at, sem("far_s", dz), sem("far", dz, h), z - dz, p, c)

    def g_far_in(dz, h):
        at = part(number(z + dz, p, c), h)
        return remote(at, at, sem("far_s", dz), sem("far", dz, h), z + dz, p, c)

    def g_own(q):
        at = whole(me)
        return remote(at, at, sem("own_s", q), sem("own", q), z, mates[q], c)

    def g_own_in(q):
        at = whole(number(z, mates[q], c))
        return remote(at, at, sem("own_s", q), sem("own", q), z, mates[q], c)

    def g_mate(dz, q, h):
        at = part(number(z + dz, p, c), h)
        return remote(at, at, sem("above_s", dz), sem("mate", dz, q, h), z, mates[q], c)

    def g_mate_in(dz, q, h):
        at = part(number(z + dz, mates[q], c), h)
        return remote(at, at, sem("above_s", dz), sem("mate", dz, q, h), z, mates[q], c)

    def g_down(q):
        at = whole(number(z, mates[q], c))
        return remote(at, at, sem("next_s"), sem("down", q), z - 1, p, c)

    def g_down_in(q):
        at = whole(number(z + 1, mates[q], c))
        return remote(at, at, sem("next_s"), sem("down", q), z + 1, p, c)

    def g_diag(dz):
        at = part(number(z, mates[3], c), 1)
        return remote(at, at, sem("far_s", dz), sem("diag", dz), z - dz, p, c)

    def g_diag_in(dz):
        at = part(number(z + dz, mates[3], c), 1)
        return remote(at, at, sem("far_s", dz), sem("diag", dz), z + dz, p, c)

    def g_core(dz, q):
        at = whole(number(z + dz, mates[q], c))
        if dz == 0:
            pair = sem("core0_s", q), sem("core0", q)
        else:
            pair = sem("above_s", dz), sem("core", dz)
        return remote(at, at, *pair, z, p, 1 - c)

    def arrived(count, name):
        span = gathered.at[pl.ds(0, count), pl.ds(0, size // 2)]
        remote(span, span, sem(*name), sem(*name), z, p, 1 - c).wait_recv()

    def left(count, name):
        span = gathered.at[pl.ds(0, count), pl.ds(0, size // 2)]
        remote(span, span, sem(*name), sem(*name), z, p, 1 - c).wait_send()

    def down_to(q):
        return (z > 0) | (mates[q] < p)

    def up_to(q):
        return (z > 0) | (mates[q] > p)

    def r_pair(dz):
        span = pl.ds(dz * PLANE, PLANE)
        return remote(
            pair_send.at[span], pair_recv.at[span], sem("reduce_s", dz), sem("pair", dz), z, p, 1 - c
        )

    def r_own(q, h):
        at = (q, pl.ds(h * columns, columns))
        return remote(
            mate_send.at[at], mate_recv.at[at], sem("share_s", q), sem("share", q), z, mates[q], c
        )

    def r_mate(dz, q, h):
        at = (dz * PLANE + q, pl.ds(h * columns, columns))
        return remote(
            mate_send.at[at], mate_recv.at[at], sem("reduce_s", dz), sem("r_mate", dz, h), z, mates[q], c
        )

    def r_up(q):
        return remote(up_send.at[q], up_recv.at[q], sem("reduce_s", 1), sem("up", q), z + 1, p, c)

    def r_diag(dz):
        return remote(
            diag_send.at[dz], diag_recv.at[dz], sem("reduce_s", dz), sem("r_diag", dz), z + dz, p, c
        )

    def r_far(dz, h):
        at = (dz, pl.ds(h * columns, columns))
        return remote(far_send.at[at], far_recv.at[at], sem("reduce_s", dz), sem("r_far", dz), z + dz, p, c)

    def decode(word):
        return word // 8, (word // 4) % 2, (word // 2) % 2, word % 2

    nothing = jnp.zeros((columns, size), jnp.bfloat16)

    def mirror_sums(device):
        sums = None
        for j in range(per_peer):
            slot, row, col, live = decode(code[device * per_peer + j])
            rows = lax.select(row == 1, turned[columns:], turned[:columns])
            left = jnp.concatenate(
                [
                    lax.select(live * (1 - col) == 1, rows, nothing),
                    lax.select(live * col == 1, rows, nothing),
                ],
                axis=0,
            )
            product = jnp.dot(left, blocks[slot], preferred_element_type=jnp.float32)
            sums = product if sums is None else sums + product
        return sums

    def give(dz):
        for pp in range(PLANE):
            pair_send[dz * PLANE + pp] = mirror_sums(number(z + dz, pp, 1 - c)).astype(
                jnp.bfloat16
            )
        r_pair(dz).start()

    def keep(dz):
        r_pair(dz).wait_recv()
        for q in others + (0,):
            pp = mates[q]
            value = mirror_sums(number(z + dz, pp, c)) + pair_recv[dz * PLANE + pp].astype(
                jnp.float32
            )
            if dz == 0:
                own_sum[q] = value
            elif dz == 1:
                up_send[q] = value.astype(jnp.bfloat16)
                if q:
                    r_up(q).start()
            elif q == 0:
                column[dz] = value
            elif q == 3:
                mate_send[dz * PLANE + q, :columns] = value[:columns].astype(jnp.bfloat16)
                diag_send[dz] = value[columns:].astype(jnp.bfloat16)
            else:
                mate_send[dz * PLANE + q] = value.astype(jnp.bfloat16)
        if dz >= 2:
            for h in range(2):
                for q in halves[h]:
                    r_mate(dz, q, h).start()
            r_diag(dz).start()

    def send_own(q, h):
        at = (q, pl.ds(h * columns, columns))
        mate_send[at] = own_sum[at].astype(jnp.bfloat16)
        r_own(q, h).start()

    def pass_far(dz, h):
        at = pl.ds(h * columns, columns)
        total = column[dz, at]
        arrived(len(halves[h]), ("r_mate", dz, h))
        for q in halves[h]:
            total = total + mate_recv[dz * PLANE + q, at].astype(jnp.float32)
        far_send[dz, at] = total.astype(jnp.bfloat16)
        r_far(dz, h).start()

    lane = lax.broadcasted_iota(jnp.int32, (size, both), 1)
    sides = [
        jnp.where((lane >= columns) == bool(kind), 1.0, 0.0).astype(jnp.bfloat16)
        for kind in range(KINDS)
    ]
    neither = jnp.zeros((size, both), jnp.bfloat16)

    def forward_sums(zz, pp, lanes):
        sums = None
        for cc in lanes:
            device = number(zz, pp, cc)
            straight = gathered[device]
            crossed = jnp.concatenate([straight[:, columns:], straight[:, :columns]], axis=1)
            for j in range(per_peer):
                slot, row, col, live = decode(code[device * per_peer + j])
                side = lax.select(
                    live * (1 - row) == 1,
                    sides[0],
                    lax.select(live * row == 1, sides[1], neither),
                )
                right = lax.select(row == col, straight, crossed) * side
                product = jnp.dot(blocks[slot], right, preferred_element_type=jnp.float32)
                sums = product if sums is None else sums + product
        return sums

    def forward(dz, lane_at=None):
        if dz == 0:

            def one(pp, _):
                @when((z > 0) | (pp >= p))
                def _():
                    forward_sum[...] = forward_sum[...] + forward_sums(z, pp, (0, 1))

                return 0

            lax.fori_loop(0, PLANE, one, 0)
        else:
            sums = forward_sum[...]
            for pp in range(PLANE):
                sums = sums + forward_sums(z + dz, pp, (lane_at,))
            forward_sum[...] = sums

    far = list(range(planes - 1, 1, -1))

    for iteration in range(ITERS):
        last = iteration == ITERS - 1
        if iteration:
            gathered[me] = turned[...].T
        for h in range(2):
            for dz in far:
                when(below(dz))(lambda dz=dz, h=h: g_far(dz, h).start())
        for q in others:
            when(down_to(q))(lambda q=q: g_own(q).start())
        g_core(0, 0).start()
        forward_sum[...] = jnp.zeros_like(forward_sum)
        if iteration == 0:
            for copy in loads:
                copy.wait()
        steps = ([("give", 1)] if planes > 1 else []) + [("give", dz) for dz in far[:1]]
        steps += [("keep", 1)] if planes > 1 else []
        for dz, after in zip(far, far[1:] + [0]):
            steps += [("give", after), ("keep", dz)]
        steps += ([] if far else [("give", 0)]) + [("keep", 0)]
        for what, dz in steps:
            when(above(dz))(lambda dz=dz, what=what: (give if what == "give" else keep)(dz))
            if (what, dz) == ("keep", 1):
                when(z > 0)(lambda: g_next().start())
        if planes > 1:
            when(above(1))(lambda: r_up(0).start())

        @when(z == 0)
        def _():
            for q in others:
                for h in range(2):
                    when(up_to(q))(lambda q=q, h=h: send_own(q, h))

        for h in range(2):
            for dz in far:

                @when(above(dz))
                def _(dz=dz, h=h):
                    g_far_in(dz, h).wait_recv()
                    for q in halves[h]:
                        g_mate(dz, q, h).start()
                    if h == 1:
                        g_core(dz, 0).start()

        for q in others:

            @when(up_to(q))
            def _(q=q):
                g_own_in(q).wait_recv()

                @when(z > 0)
                def _():
                    g_down(q).start()

                if q == 3:
                    for dz in far:
                        when(below(dz))(lambda dz=dz: g_diag(dz).start())

                g_core(0, q).start()

        @when(z > 0)
        def _():
            for q in others:
                r_up(q).wait_recv()
                own_sum[q] = own_sum[q] + up_recv[q].astype(jnp.float32)
                send_own(q, 0)
                if q == 3:
                    for dz in far:

                        @when(below(dz))
                        def _(dz=dz):
                            r_diag(dz).wait_recv()
                            at = (q, pl.ds(columns, columns))
                            own_sum[at] = own_sum[at] + diag_recv[dz].astype(jnp.float32)

                send_own(q, 1)

        for dz in far:
            for h in range(2):
                when(above(dz))(lambda dz=dz, h=h: pass_far(dz, h))

        arrived(2, ("core0", 0))
        for q in others:
            when(up_to(q))(lambda q=q: arrived(2, ("core0", q)))
        forward(0)

        if planes > 1:

            @when(above(1))
            def _():
                g_next_in().wait_recv()
                g_core(1, 0).start()
                for q in others:
                    g_down_in(q).wait_recv()
                    g_core(1, q).start()
                forward(1, c)
                arrived(2 * PLANE, ("core", 1))
                forward(1, 1 - c)

        def other_lane(dz):
            arrived(2 * PLANE, ("core", dz))
            forward(dz, 1 - c)

        for dz in far:

            @when(above(dz))
            def _(dz=dz):
                for q in others:
                    for h in range(2):
                        if q in halves[h]:
                            g_mate_in(dz, q, h).wait_recv()
                        else:
                            g_diag_in(dz).wait_recv()
                    g_core(dz, q).start()
                forward(dz, c)
                if dz < planes - 1:
                    when(above(dz + 1))(lambda: other_lane(dz + 1))

        if far:
            when(above(2))(lambda: other_lane(2))

        if planes > 1:
            when(z > 0)(lambda: left(2 * PLANE, ("next_s",)))
        for dz in far:
            when(below(dz))(lambda dz=dz: left(3, ("far_s", dz)))
        left(2, ("core0_s", 0))
        for q in others:
            when(down_to(q))(lambda q=q: left(2, ("own_s", q)))
            when(up_to(q))(lambda q=q: left(2, ("core0_s", q)))
        for dz in range(1, planes):
            count = 2 * PLANE + (len(halves[0]) + len(halves[1]) if dz >= 2 else 0)
            when(above(dz))(lambda dz=dz, count=count: left(count, ("above_s", dz)))

        image[...] = forward_sum[...].T + own_sum[0]

        @when(z > 0)
        def _():
            r_up(0).wait_recv()
            image[...] = image[...] + up_recv[0].astype(jnp.float32)

        for q in others:

            @when(down_to(q))
            def _(q=q):
                arrived(2, ("share", q))
                image[...] = image[...] + mate_recv[q].astype(jnp.float32)

        for dz in range(2, planes):

            @when(below(dz))
            def _(dz=dz):
                arrived(2, ("r_far", dz))
                image[...] = image[...] + far_recv[dz].astype(jnp.float32)

        rows = image[...]

        def diagonal_sum(square):
            return square[:columns, :columns] + square[columns:, columns:]

        gram = diagonal_sum(nt_dot(rows, rows, HIGH))
        half = columns // 2
        tall = columns if last else half
        peers = 2 * PLANE - 1
        base = iteration * 2
        rbase = iteration * (peers + planes - 1)
        line[base, :half] = fold(gram)
        if last:
            line[base, half:] = fold(diagonal_sum(nt_dot(turned[...].astype(jnp.float32), rows, HIGH)))
        copies = []
        for i, (zz, pp, cc) in enumerate(greeted[:peers]):
            copies.append(
                remote(
                    line.at[base, pl.ds(0, tall)], line_recv.at[rbase + i, pl.ds(0, tall)],
                    sem("plane_s", iteration), sem("plane", iteration), zz, pp, cc,
                )
            )
        for copy in copies:
            copy.start()
        for q in others:
            when(up_to(q))(lambda q=q: left(2, ("share_s", q)))
        for dz in range(planes):
            count = 2 * PLANE
            if dz == 1:
                count += 2 * PLANE
            if dz >= 2:
                count += len(halves[0]) + len(halves[1]) + 3
            when(above(dz))(lambda dz=dz, count=count: left(count, ("reduce_s", dz)))

        total = line[base, :tall]
        span = line_recv.at[pl.ds(rbase, peers), pl.ds(0, tall)]
        remote(span, span, sem("plane_s", iteration), sem("plane", iteration), z, p, 1 - c).wait()
        for i in range(peers):
            total = total + line_recv[rbase + i, :tall]
        line[base + 1, :tall] = total
        def column_wait(piece):
            name = ("gram", "proj")[piece]
            span = line_recv.at[pl.ds(rbase + peers, planes - 1), pl.ds(piece * half, half)]
            remote(span, span, sem(name + "_s", iteration), sem(name, iteration), z, p, 1 - c).wait()

        for piece in range(2 if last else 1):
            span = pl.ds(piece * half, half)
            for s in range(1, planes):
                name = ("gram", "proj")[piece]
                copy = remote(
                    line.at[base + 1, span], line_recv.at[rbase + peers + s - 1, span],
                    sem(name + "_s", iteration), sem(name, iteration), (z + s) % planes, p, c,
                )
                copy.start()
        column_wait(0)
        summed = line[base + 1, :half]
        for s in range(1, planes):
            summed = summed + line_recv[rbase + peers + s - 1, :half]
        summed = unfold(summed / total_rows)
        inverse = inverse_factor(summed, columns)
        if last:
            inverse_ref[...] = inverse
            column_wait(1)
            summed = line[base + 1, half:]
            for s in range(1, planes):
                summed = summed + line_recv[rbase + peers + s - 1, half:]
            proj_ref[...] = unfold(summed)
        for kind in range(KINDS):
            at = pl.ds(kind * columns, columns)
            if last:
                embed_ref[:, kind * size : (kind + 1) * size] = image[at]
            else:
                result = jnp.dot(
                    inverse, image[at], precision=HIGH, preferred_element_type=jnp.float32
                )
                turned[at] = result.astype(jnp.bfloat16)


def closing(total_rows, image_ref, inverse_ref, sum_ref, embed_ref, proj_ref):
    embed_ref[...] = jnp.dot(
        inverse_ref[...], image_ref[...], precision=HIGH, preferred_element_type=jnp.float32
    )
    proj_ref[...] = sum_ref[...] / total_rows


def on_device(start_basis, kernel_blocks, block_row, block_col, block_count):
    devices = lax.axis_size("rows") * lax.axis_size("grp")
    me = lax.axis_index("rows") * lax.axis_size("grp") + lax.axis_index("grp")
    slots, size, _ = kernel_blocks.shape
    own_rows, columns = start_basis.shape
    per_peer = (slots + devices - 1) // devices
    planes = lax.axis_size("rows") // PLANE
    total_rows = own_rows * devices

    positions = jnp.arange(slots, dtype=jnp.int32)
    alive = positions < block_count[0]
    local_row = jnp.clip(block_row - me * KINDS, 0, KINDS - 1)
    target = block_col // KINDS
    earlier = (
        (target[:, None] == target[None, :])
        & alive[None, :]
        & (positions[None, :] < positions[:, None])
    )
    rank = jnp.sum(earlier.astype(jnp.int32), axis=1)
    spot = jnp.where(alive, target * per_peer + rank, -1)
    hit = spot[None, :] == jnp.arange(devices * per_peer, dtype=jnp.int32)[:, None]
    word = positions * 8 + local_row * 4 + (block_col - target * KINDS) * 2 + 1
    code = jnp.sum(jnp.where(hit, word[None, :], 0), axis=1)

    smem = pl.BlockSpec(memory_space=pltpu.SMEM)
    vmem = pl.BlockSpec(memory_space=pltpu.VMEM)
    dma = pltpu.SemaphoreType.DMA
    peers = 2 * PLANE - 1
    both = KINDS * columns

    def halves(*lead):
        return pltpu.VMEM((*lead, both, size), jnp.bfloat16)

    def singles(*lead):
        return pltpu.VMEM((*lead, both, size), jnp.float32)

    image, projected, inverse = pl.pallas_call(
        functools.partial(kernel, planes, total_rows, per_peer, columns),
        out_shape=(
            jax.ShapeDtypeStruct((columns, own_rows), jnp.float32),
            jax.ShapeDtypeStruct((columns, columns), jnp.float32),
            jax.ShapeDtypeStruct((columns, columns), jnp.float32),
        ),
        in_specs=[smem, vmem, pl.BlockSpec(memory_space=pl.ANY)],
        out_specs=(vmem, vmem, vmem),
        scratch_shapes=[
            pltpu.VMEM((slots, size, size), jnp.bfloat16),
            halves(),
            pltpu.VMEM((devices, size, both), jnp.bfloat16),
            halves(planes * PLANE),
            halves(planes * PLANE),
            halves(planes * PLANE),
            halves(planes * PLANE),
            halves(PLANE),
            halves(PLANE),
            pltpu.VMEM((planes, columns, size), jnp.bfloat16),
            pltpu.VMEM((planes, columns, size), jnp.bfloat16),
            halves(planes),
            halves(planes),
            singles(planes),
            singles(PLANE),
            pltpu.VMEM((size, both), jnp.float32),
            singles(),
            pltpu.VMEM((ITERS * 2, columns, 2 * columns), jnp.float32),
            pltpu.VMEM((ITERS * (peers + planes - 1), columns, 2 * columns), jnp.float32),
            dma((CHUNKS,)),
            dma((len(semaphores(planes)),)),
        ],
        compiler_params=pltpu.CompilerParams(
            collective_id=0, has_side_effects=True, vmem_limit_bytes=62 * 1024 * 1024
        ),
    )(code, start_basis.T, kernel_blocks)
    embedded, projected = pl.pallas_call(
        functools.partial(closing, total_rows),
        out_shape=(
            jax.ShapeDtypeStruct((columns, own_rows), jnp.float32),
            jax.ShapeDtypeStruct((columns, columns), jnp.float32),
        ),
        in_specs=[vmem] * 3,
        out_specs=(vmem, vmem),
    )(image, inverse, projected)
    return embedded.T, projected


def solution(mesh):
    in_specs = (
        P(("rows", "grp"), None),
        P(("rows", "grp"), None, None),
        P(("rows", "grp")),
        P(("rows", "grp")),
        P(("rows", "grp")),
    )
    out_specs = (P(("rows", "grp"), None), P())
    return jax.shard_map(
        on_device, mesh=mesh, in_specs=in_specs, out_specs=out_specs, check_vma=False
    )
```

```python
import functools

import jax
import jax.numpy as jnp
from jax import lax
from jax.experimental import pallas as pl
from jax.experimental.pallas import tpu as pltpu
from jax.sharding import PartitionSpec as P

ITERS = 2
PLANE = 4
KINDS = 2
MESH = pl.DeviceIdType.MESH
HIGH = lax.Precision.HIGHEST
CHUNKS = 4
SPLIT_FROM = 2


def whole_diagonal(dz):
    return dz >= 3


def split_even(total, parts):
    edges = [total * i // parts for i in range(parts + 1)]
    return list(zip(edges[:-1], edges[1:]))


def nt_dot(a, b, precision=None):
    return lax.dot_general(
        a, b, (((1,), (1,)), ((), ())), preferred_element_type=jnp.float32, precision=precision
    )


def inverse_root(value):
    guess = lax.rsqrt(value)
    return guess * (1.5 - 0.5 * (value * guess) * guess)


def inverse_factor(gram, columns):
    tall = 8
    wide = 2 * columns
    row_id = lax.broadcasted_iota(jnp.int32, (columns, wide), 0)
    lane_id = lax.broadcasted_iota(jnp.int32, (columns, wide), 1)
    both = jnp.concatenate([gram, gram], axis=1)
    on_diagonal = (lane_id == row_id) | (lane_id == row_id + columns)
    diagonal = jnp.where(on_diagonal, both, 0.0)
    across = inverse_root(jnp.sum(diagonal, axis=0, keepdims=True))
    down = inverse_root(0.5 * jnp.sum(diagonal, axis=1, keepdims=True))
    unit = jnp.where(lane_id == row_id + columns, 1.0, 0.0).astype(jnp.float32)
    work = jnp.where(lane_id < columns, both * down * across, unit)
    tiles = [work[i : i + tall] for i in range(0, columns, tall)]

    def spread(row):
        return jnp.broadcast_to(row, (tall, wide))

    done = []
    for t in range(len(tiles)):
        k = t * tall
        cols = [
            [jnp.broadcast_to(tile[:, k + j : k + j + 1], (tall, wide)) for tile in tiles[t:]]
            for j in range(tall)
        ]
        rows = [spread(tiles[t][i : i + 1]) for i in range(tall)]
        p = [[spread(cols[j][0][i : i + 1]) for j in range(i + 1)] for i in range(tall)]
        inv = [None] * tall
        for j in range(0, tall, 2):
            det = p[j][j] * p[j + 1][j + 1] - p[j + 1][j] * p[j + 1][j]
            inv[j] = 1.0 / p[j][j]
            inv[j + 1] = p[j][j] * (1.0 / det)
            lead = p[j + 1][j] * inv[j]
            rows[j + 1] = rows[j + 1] - lead * rows[j]
            cols[j + 1] = [c1 - lead * c0 for c1, c0 in zip(cols[j + 1], cols[j])]
            p[j + 1][j + 1] = p[j + 1][j + 1] - lead * p[j + 1][j]
            for i in range(j + 2, tall):
                p[i][j + 1] = p[i][j + 1] - lead * p[i][j]
            for i in range(j + 2, tall):
                l0, l1 = p[i][j] * inv[j], p[i][j + 1] * inv[j + 1]
                rows[i] = rows[i] - l0 * rows[j] - l1 * rows[j + 1]
                cols[i] = [
                    ci - l0 * c0 - l1 * c1 for ci, c0, c1 in zip(cols[i], cols[j], cols[j + 1])
                ]
                for m in range(i, tall):
                    p[m][i] = p[m][i] - l0 * p[m][j] - l1 * p[m][j + 1]
        for i in range(tall):
            done.append((rows[i] * inverse_root(p[i][i]))[:1])
        scaled = [rows[i] * inv[i] for i in range(tall)]
        for at in range(t + 1, len(tiles)):
            for i in range(tall):
                tiles[at] = tiles[at] - cols[i][at - t] * scaled[i]
    return (jnp.concatenate(done, axis=0) * across)[:, columns:]


def fold(square):
    half = square.shape[0] // 2
    return jnp.concatenate([square[:half], square[half:]], axis=1)


def unfold(packed):
    half = packed.shape[1] // 2
    return jnp.concatenate([packed[:, :half], packed[:, half:]], axis=0)


def halves(dz):
    if whole_diagonal(dz):
        return ((1, 2), (1, 2))
    return ((3, 1, 2), (1, 2) if dz >= SPLIT_FROM else (3, 1, 2))


def semaphores(planes):
    far, others = range(2, planes), range(1, PLANE)
    names = ["next", "next_s"]
    for iteration in range(ITERS):
        names += [(stage + side, iteration) for stage in ("plane", "gram", "proj") for side in ("", "_s")]
    names += [("own", q) for q in others] + [("own_s", q) for q in others]
    names += [("down", q) for q in others] + [("core0", q) for q in range(PLANE)]
    names += [("core0_s", q) for q in range(PLANE)] + [("up", q) for q in range(PLANE)]
    names += [("share", q) for q in others] + [("share_s", q) for q in others]
    names += [("core", dz) for dz in range(1, planes)] + [("above_s", dz) for dz in range(1, planes)]
    names += [("pair", dz) for dz in range(planes)] + [("reduce_s", dz) for dz in range(planes)]
    for dz in far:
        names += [(name, dz) for name in ("far_s", "diag", "r_diag", "r_far")]
        names += [(name, dz, h) for name in ("far", "r_mate") for h in range(2)]
        names += [("mate", dz, q, h) for h in range(2) for q in halves(dz)[h]]
    return {name: i for i, name in enumerate(names)}


def slot_table(row_ref, col_ref, count, first_row, per_peer, places):
    slots = row_ref.shape[1]
    square = (slots, slots)
    down = lax.broadcasted_iota(jnp.int32, square, 0)
    across = lax.broadcasted_iota(jnp.int32, square, 1)
    position = lax.broadcasted_iota(jnp.int32, (1, slots), 1)

    def turn(row):
        spread = jnp.broadcast_to(row, square)
        return jnp.sum(jnp.where(down == across, spread, 0), axis=1, keepdims=True)

    target = lax.div(col_ref[...], KINDS)
    local_row = jnp.clip(row_ref[...] - first_row, 0, KINDS - 1)
    word = position * 8 + local_row * 4 + (col_ref[...] - target * KINDS) * 2 + 1
    key = jnp.where(position < count, target, -1)
    key_down, word_down = turn(key), turn(word)
    earlier = (key_down == key) & (across < down)
    rank = jnp.sum(jnp.where(earlier, 1, 0), axis=1, keepdims=True)
    spot = jnp.where(key_down >= 0, key_down * per_peer + rank, -1)
    hit = spot == lax.broadcasted_iota(jnp.int32, (slots, places), 1)
    return jnp.sum(jnp.where(hit, word_down, 0), axis=0, keepdims=True)


def kernel(
    planes, total_rows, per_peer, columns,
    row_ref, col_ref, count_ref, start_ref, blocks_hbm, embed_ref, proj_ref, inverse_ref,
    blocks, turned, gathered, pair_send, pair_recv, mate_send, mate_recv,
    up_send, up_recv, diag_send, diag_recv, far_send, far_recv, column, own_sum, forward_sum, image, line, line_recv,
    code_vector, code, load_sem, code_sem, sems,
):
    size, both = gathered.shape[1:]
    slots = blocks.shape[0]
    rows_at = lax.axis_index("rows")
    c = lax.axis_index("grp")
    z = rows_at // PLANE
    p = rows_at % PLANE
    px, py = p % 2, p // 2

    def mate(q):
        x = px + (q % 2) * (1 - 2 * px)
        y = py + (q // 2) * (1 - 2 * py)
        return 2 * y + x

    mates = [mate(q) for q in range(PLANE)]
    places = semaphores(planes)

    def sem(*name):
        return sems.at[places[name if len(name) > 1 else name[0]]]
    others = (1, 2, 3)

    def number(zz, pp, cc):
        return (zz * PLANE + pp) * 2 + cc

    def remote(src, dst, s, r, zz, pp, cc):
        return pltpu.make_async_remote_copy(
            src, dst, s, r, device_id=(zz * PLANE + pp, cc), device_id_type=MESH
        )

    loads = [
        pltpu.make_async_copy(
            blocks_hbm.at[pl.ds(lo, hi - lo)], blocks.at[pl.ds(lo, hi - lo)], load_sem.at[i]
        )
        for i, (lo, hi) in enumerate(split_even(slots, CHUNKS))
    ]
    for copy in loads:
        copy.start()
    barrier = pltpu.get_barrier_semaphore()
    greeted = [(z, mates[q], 1 - c if f else c) for q in range(PLANE) for f in (0, 1) if q or f]
    greeted += [((z + s) % planes, p, c) for s in range(1, planes)]
    for zz, pp, cc in greeted:
        pl.semaphore_signal(barrier, inc=1, device_id=(zz * PLANE + pp, cc), device_id_type=MESH)
    turned[...] = jnp.concatenate([start_ref[:, :size], start_ref[:, size:]], axis=0)
    gathered[number(z, p, c)] = turned[...].T
    code_vector[...] = slot_table(
        row_ref, col_ref, count_ref[0], number(z, p, c) * KINDS, per_peer, code_vector.shape[1]
    )
    code_copy = pltpu.make_async_copy(code_vector, code, code_sem.at[0])
    code_copy.start()
    pl.semaphore_wait(barrier, len(greeted))

    def above(dz):
        return z + dz < planes

    def below(dz):
        return z - dz >= 0

    when = pl.when
    me = number(z, p, c)

    def whole(device):
        return gathered.at[device]

    def part(device, h):
        return gathered.at[device, pl.ds(h * (size // 2), size // 2)]

    def g_next():
        at = whole(me)
        return remote(at, at, sem("next_s"), sem("next"), z - 1, p, c)

    def g_next_in():
        at = whole(number(z + 1, p, c))
        return remote(at, at, sem("next_s"), sem("next"), z + 1, p, c)

    def g_far(dz, h):
        at = part(me, h)
        return remote(at, at, sem("far_s", dz), sem("far", dz, h), z - dz, p, c)

    def g_far_in(dz, h):
        at = part(number(z + dz, p, c), h)
        return remote(at, at, sem("far_s", dz), sem("far", dz, h), z + dz, p, c)

    def g_own(q):
        at = whole(me)
        return remote(at, at, sem("own_s", q), sem("own", q), z, mates[q], c)

    def g_own_in(q):
        at = whole(number(z, mates[q], c))
        return remote(at, at, sem("own_s", q), sem("own", q), z, mates[q], c)

    def g_mate(dz, q, h):
        at = part(number(z + dz, p, c), h)
        return remote(at, at, sem("above_s", dz), sem("mate", dz, q, h), z, mates[q], c)

    def g_mate_in(dz, q, h):
        at = part(number(z + dz, mates[q], c), h)
        return remote(at, at, sem("above_s", dz), sem("mate", dz, q, h), z, mates[q], c)

    def g_down(q):
        at = whole(number(z, mates[q], c))
        return remote(at, at, sem("next_s"), sem("down", q), z - 1, p, c)

    def g_down_in(q):
        at = whole(number(z + 1, mates[q], c))
        return remote(at, at, sem("next_s"), sem("down", q), z + 1, p, c)

    def diagonal(dz, device):
        return whole(device) if whole_diagonal(dz) else part(device, 1)

    def g_diag(dz):
        at = diagonal(dz, number(z, mates[3], c))
        return remote(at, at, sem("far_s", dz), sem("diag", dz), z - dz, p, c)

    def g_diag_in(dz):
        at = diagonal(dz, number(z + dz, mates[3], c))
        return remote(at, at, sem("far_s", dz), sem("diag", dz), z + dz, p, c)

    def g_core(dz, q):
        at = whole(number(z + dz, mates[q], c))
        if dz == 0:
            pair = sem("core0_s", q), sem("core0", q)
        else:
            pair = sem("above_s", dz), sem("core", dz)
        return remote(at, at, *pair, z, p, 1 - c)

    def arrived(count, name):
        span = gathered.at[pl.ds(0, count), pl.ds(0, size // 2)]
        remote(span, span, sem(*name), sem(*name), z, p, 1 - c).wait_recv()

    def left(count, name):
        span = gathered.at[pl.ds(0, count), pl.ds(0, size // 2)]
        remote(span, span, sem(*name), sem(*name), z, p, 1 - c).wait_send()

    def down_to(q):
        return (z > 0) | (mates[q] < p)

    def up_to(q):
        return (z > 0) | (mates[q] > p)

    def r_pair(dz):
        span = pl.ds(dz * PLANE, PLANE)
        return remote(
            pair_send.at[span], pair_recv.at[span], sem("reduce_s", dz), sem("pair", dz), z, p, 1 - c
        )

    def r_own(q, h):
        at = (q, pl.ds(h * columns, columns))
        return remote(
            mate_send.at[at], mate_recv.at[at], sem("share_s", q), sem("share", q), z, mates[q], c
        )

    def r_mate(dz, q, h):
        at = (dz * PLANE + q, pl.ds(h * columns, columns))
        return remote(
            mate_send.at[at], mate_recv.at[at], sem("reduce_s", dz), sem("r_mate", dz, h), z, mates[q], c
        )

    def r_up(q):
        return remote(up_send.at[q], up_recv.at[q], sem("reduce_s", 1), sem("up", q), z + 1, p, c)

    def r_diag(dz):
        at = (dz,) if whole_diagonal(dz) else (dz, pl.ds(columns, columns))
        return remote(
            diag_send.at[at], diag_recv.at[at], sem("reduce_s", dz), sem("r_diag", dz), z + dz, p, c
        )

    def r_far(dz, h):
        at = (dz, pl.ds(h * columns, columns))
        return remote(far_send.at[at], far_recv.at[at], sem("reduce_s", dz), sem("r_far", dz), z + dz, p, c)

    def decode(word):
        return word // 8, (word // 4) % 2, (word // 2) % 2, word % 2

    nothing = jnp.zeros((columns, size), jnp.bfloat16)

    def mirror_sums(device):
        sums = None
        for j in range(per_peer):
            slot, row, col, live = decode(code[0, device * per_peer + j])
            rows = lax.select(row == 1, turned[columns:], turned[:columns])
            left = jnp.concatenate(
                [
                    lax.select(live * (1 - col) == 1, rows, nothing),
                    lax.select(live * col == 1, rows, nothing),
                ],
                axis=0,
            )
            product = jnp.dot(left, blocks[slot], preferred_element_type=jnp.float32)
            sums = product if sums is None else sums + product
        return sums

    def give(dz):
        for pp in range(PLANE):
            pair_send[dz * PLANE + pp] = mirror_sums(number(z + dz, pp, 1 - c)).astype(
                jnp.bfloat16
            )
        r_pair(dz).start()

    def keep(dz):
        r_pair(dz).wait_recv()
        for q in others + (0,):
            pp = mates[q]
            value = mirror_sums(number(z + dz, pp, c)) + pair_recv[dz * PLANE + pp].astype(
                jnp.float32
            )
            if dz == 0:
                own_sum[q] = value
            elif dz == 1:
                up_send[q] = value.astype(jnp.bfloat16)
                if q:
                    r_up(q).start()
            elif q == 0:
                column[dz] = value
            elif q == 3 and dz >= SPLIT_FROM:
                mate_send[dz * PLANE + q] = value.astype(jnp.bfloat16)
                diag_send[dz] = value.astype(jnp.bfloat16)
            else:
                mate_send[dz * PLANE + q] = value.astype(jnp.bfloat16)
        if dz >= 2:
            for h in range(2):
                for q in halves(dz)[h]:
                    r_mate(dz, q, h).start()
            if dz >= SPLIT_FROM:
                r_diag(dz).start()

    def send_own(q, h):
        at = (q, pl.ds(h * columns, columns))
        mate_send[at] = own_sum[at].astype(jnp.bfloat16)
        r_own(q, h).start()

    def pass_far(dz, h):
        at = pl.ds(h * columns, columns)
        total = column[dz, at]
        arrived(len(halves(dz)[h]), ("r_mate", dz, h))
        for q in halves(dz)[h]:
            total = total + mate_recv[dz * PLANE + q, at].astype(jnp.float32)
        far_send[dz, at] = total.astype(jnp.bfloat16)
        r_far(dz, h).start()

    lane = lax.broadcasted_iota(jnp.int32, (size, both), 1)
    sides = [
        jnp.where((lane >= columns) == bool(kind), 1.0, 0.0).astype(jnp.bfloat16)
        for kind in range(KINDS)
    ]
    neither = jnp.zeros((size, both), jnp.bfloat16)

    def forward_sums(zz, pp, lanes):
        sums = None
        for cc in lanes:
            device = number(zz, pp, cc)
            straight = gathered[device]
            crossed = jnp.concatenate([straight[:, columns:], straight[:, :columns]], axis=1)
            for j in range(per_peer):
                slot, row, col, live = decode(code[0, device * per_peer + j])
                side = lax.select(
                    live * (1 - row) == 1,
                    sides[0],
                    lax.select(live * row == 1, sides[1], neither),
                )
                right = lax.select(row == col, straight, crossed) * side
                product = jnp.dot(blocks[slot], right, preferred_element_type=jnp.float32)
                sums = product if sums is None else sums + product
        return sums

    def forward(dz, lane_at=None):
        if dz == 0:

            def one(pp, _):
                @when((z > 0) | (pp >= p))
                def _():
                    forward_sum[...] = forward_sum[...] + forward_sums(z, pp, (0, 1))

                return 0

            lax.fori_loop(0, PLANE, one, 0)
        else:
            sums = forward_sum[...]
            for pp in range(PLANE):
                sums = sums + forward_sums(z + dz, pp, (lane_at,))
            forward_sum[...] = sums

    def far_count(dz):
        return 2 + (2 if whole_diagonal(dz) else int(dz >= SPLIT_FROM))

    far = list(range(planes - 1, 1, -1))
    far_split = [dz for dz in far if dz >= SPLIT_FROM]

    for iteration in range(ITERS):
        last = iteration == ITERS - 1
        if iteration:
            gathered[me] = turned[...].T
        for h in range(2):
            for dz in far:
                when(below(dz))(lambda dz=dz, h=h: g_far(dz, h).start())
        for q in others:
            when(down_to(q))(lambda q=q: g_own(q).start())
        g_core(0, 0).start()
        forward_sum[...] = jnp.zeros_like(forward_sum)
        if iteration == 0:
            code_copy.wait()
            for copy in loads:
                copy.wait()
        steps = ([("give", 1)] if planes > 1 else []) + [("give", dz) for dz in far[:1]]
        steps += [("keep", 1)] if planes > 1 else []
        for dz, after in zip(far, far[1:] + [0]):
            steps += [("give", after), ("keep", dz)]
        steps += ([] if far else [("give", 0)]) + [("keep", 0)]
        for what, dz in steps:
            when(above(dz))(lambda dz=dz, what=what: (give if what == "give" else keep)(dz))
            if (what, dz) == ("keep", 1):
                when(z > 0)(lambda: g_next().start())
        if planes > 1:
            when(above(1))(lambda: r_up(0).start())

        @when(z == 0)
        def _():
            for q in others:
                for h in range(2):
                    when(up_to(q))(lambda q=q, h=h: send_own(q, h))

        for h in range(2):
            for dz in far:

                @when(above(dz))
                def _(dz=dz, h=h):
                    g_far_in(dz, h).wait_recv()
                    for q in halves(dz)[h]:
                        g_mate(dz, q, h).start()
                    if h == 1:
                        g_core(dz, 0).start()

        for q in others:

            @when(up_to(q))
            def _(q=q):
                g_own_in(q).wait_recv()

                @when(z > 0)
                def _():
                    g_down(q).start()

                if q == 3:
                    for dz in far_split:
                        when(below(dz))(lambda dz=dz: g_diag(dz).start())

                g_core(0, q).start()

        @when(z > 0)
        def _():
            for q in others:
                r_up(q).wait_recv()
                own_sum[q] = own_sum[q] + up_recv[q].astype(jnp.float32)
                early = q < 3 or not any(whole_diagonal(dz) for dz in far)
                if early:
                    send_own(q, 0)
                if q == 3:
                    for dz in far_split:

                        @when(below(dz))
                        def _(dz=dz):
                            r_diag(dz).wait_recv()
                            first = 0 if whole_diagonal(dz) else columns
                            at = pl.ds(first, 2 * columns - first)
                            own_sum[q, at] = own_sum[q, at] + diag_recv[dz, at].astype(jnp.float32)

                if not early:
                    send_own(q, 0)
                send_own(q, 1)

        for dz in far:
            for h in range(2):
                when(above(dz))(lambda dz=dz, h=h: pass_far(dz, h))

        arrived(2, ("core0", 0))
        for q in others:
            when(up_to(q))(lambda q=q: arrived(2, ("core0", q)))
        forward(0)

        if planes > 1:

            @when(above(1))
            def _():
                g_next_in().wait_recv()
                g_core(1, 0).start()
                for q in others:
                    g_down_in(q).wait_recv()
                    g_core(1, q).start()
                forward(1, c)
                arrived(2 * PLANE, ("core", 1))
                forward(1, 1 - c)

        def other_lane(dz):
            arrived(2 * PLANE, ("core", dz))
            forward(dz, 1 - c)

        for dz in far:

            @when(above(dz))
            def _(dz=dz):
                for q in others:
                    for h in range(2):
                        if q in halves(dz)[h]:
                            g_mate_in(dz, q, h).wait_recv()
                    if q == 3 and dz >= SPLIT_FROM:
                        g_diag_in(dz).wait_recv()
                    g_core(dz, q).start()
                forward(dz, c)
                if dz < planes - 1:
                    when(above(dz + 1))(lambda: other_lane(dz + 1))

        if far:
            when(above(2))(lambda: other_lane(2))

        if planes > 1:
            when(z > 0)(lambda: left(2 * PLANE, ("next_s",)))
        for dz in far:
            when(below(dz))(lambda dz=dz: left(far_count(dz), ("far_s", dz)))
        left(2, ("core0_s", 0))
        for q in others:
            when(down_to(q))(lambda q=q: left(2, ("own_s", q)))
            when(up_to(q))(lambda q=q: left(2, ("core0_s", q)))
        for dz in range(1, planes):
            count = 2 * PLANE + (len(halves(dz)[0]) + len(halves(dz)[1]) if dz >= 2 else 0)
            when(above(dz))(lambda dz=dz, count=count: left(count, ("above_s", dz)))

        image[...] = forward_sum[...].T + own_sum[0]

        @when(z > 0)
        def _():
            r_up(0).wait_recv()
            image[...] = image[...] + up_recv[0].astype(jnp.float32)

        for q in others:

            @when(down_to(q))
            def _(q=q):
                arrived(2, ("share", q))
                image[...] = image[...] + mate_recv[q].astype(jnp.float32)

        for dz in range(2, planes):

            @when(below(dz))
            def _(dz=dz):
                arrived(2, ("r_far", dz))
                image[...] = image[...] + far_recv[dz].astype(jnp.float32)

        rows = image[...]

        def diagonal_sum(square):
            return square[:columns, :columns] + square[columns:, columns:]

        gram = diagonal_sum(nt_dot(rows, rows, HIGH))
        half = columns // 2
        tall = columns if last else half
        peers = 2 * PLANE - 1
        base = iteration * 2
        rbase = iteration * (peers + planes - 1)
        line[base, :half] = fold(gram)
        if last:
            line[base, half:] = fold(diagonal_sum(nt_dot(turned[...].astype(jnp.float32), rows, HIGH)))
        copies = []
        for i, (zz, pp, cc) in enumerate(greeted[:peers]):
            copies.append(
                remote(
                    line.at[base, pl.ds(0, tall)], line_recv.at[rbase + i, pl.ds(0, tall)],
                    sem("plane_s", iteration), sem("plane", iteration), zz, pp, cc,
                )
            )
        for copy in copies:
            copy.start()
        for q in others:
            when(up_to(q))(lambda q=q: left(2, ("share_s", q)))
        for dz in range(planes):
            count = 2 * PLANE
            if dz == 1:
                count += 2 * PLANE
            if dz >= 2:
                count += len(halves(dz)[0]) + len(halves(dz)[1]) + far_count(dz)
            when(above(dz))(lambda dz=dz, count=count: left(count, ("reduce_s", dz)))

        total = line[base, :tall]
        span = line_recv.at[pl.ds(rbase, peers), pl.ds(0, tall)]
        remote(span, span, sem("plane_s", iteration), sem("plane", iteration), z, p, 1 - c).wait()
        for i in range(peers):
            total = total + line_recv[rbase + i, :tall]
        line[base + 1, :tall] = total
        def column_wait(piece):
            name = ("gram", "proj")[piece]
            span = line_recv.at[pl.ds(rbase + peers, planes - 1), pl.ds(piece * half, half)]
            remote(span, span, sem(name + "_s", iteration), sem(name, iteration), z, p, 1 - c).wait()

        for piece in range(2 if last else 1):
            span = pl.ds(piece * half, half)
            for s in range(1, planes):
                name = ("gram", "proj")[piece]
                copy = remote(
                    line.at[base + 1, span], line_recv.at[rbase + peers + s - 1, span],
                    sem(name + "_s", iteration), sem(name, iteration), (z + s) % planes, p, c,
                )
                copy.start()
        column_wait(0)
        summed = line[base + 1, :half]
        for s in range(1, planes):
            summed = summed + line_recv[rbase + peers + s - 1, :half]
        summed = unfold(summed / total_rows)
        inverse = inverse_factor(summed, columns)
        if last:
            inverse_ref[...] = inverse
            column_wait(1)
            summed = line[base + 1, half:]
            for s in range(1, planes):
                summed = summed + line_recv[rbase + peers + s - 1, half:]
            proj_ref[...] = unfold(summed)
        for kind in range(KINDS):
            at = pl.ds(kind * columns, columns)
            if last:
                embed_ref[:, kind * size : (kind + 1) * size] = image[at]
            else:
                result = jnp.dot(
                    inverse, image[at], precision=HIGH, preferred_element_type=jnp.float32
                )
                turned[at] = result.astype(jnp.bfloat16)


def closing(total_rows, image_ref, inverse_ref, sum_ref, embed_ref, proj_ref):
    embed_ref[...] = jnp.dot(
        inverse_ref[...], image_ref[...], precision=HIGH, preferred_element_type=jnp.float32
    )
    proj_ref[...] = sum_ref[...] / total_rows


def on_device(start_basis, kernel_blocks, block_row, block_col, block_count):
    devices = lax.axis_size("rows") * lax.axis_size("grp")
    slots, size, _ = kernel_blocks.shape
    own_rows, columns = start_basis.shape
    per_peer = (slots + devices - 1) // devices
    planes = lax.axis_size("rows") // PLANE
    total_rows = own_rows * devices

    smem = pl.BlockSpec(memory_space=pltpu.SMEM)
    vmem = pl.BlockSpec(memory_space=pltpu.VMEM)
    dma = pltpu.SemaphoreType.DMA
    peers = 2 * PLANE - 1
    both = KINDS * columns

    def narrow(*lead):
        return pltpu.VMEM((*lead, both, size), jnp.bfloat16)

    def singles(*lead):
        return pltpu.VMEM((*lead, both, size), jnp.float32)

    image, projected, inverse = pl.pallas_call(
        functools.partial(kernel, planes, total_rows, per_peer, columns),
        out_shape=(
            jax.ShapeDtypeStruct((columns, own_rows), jnp.float32),
            jax.ShapeDtypeStruct((columns, columns), jnp.float32),
            jax.ShapeDtypeStruct((columns, columns), jnp.float32),
        ),
        in_specs=[vmem, vmem, smem, vmem, pl.BlockSpec(memory_space=pl.ANY)],
        out_specs=(vmem, vmem, vmem),
        scratch_shapes=[
            pltpu.VMEM((slots, size, size), jnp.bfloat16),
            narrow(),
            pltpu.VMEM((devices, size, both), jnp.bfloat16),
            narrow(planes * PLANE),
            narrow(planes * PLANE),
            narrow(planes * PLANE),
            narrow(planes * PLANE),
            narrow(PLANE),
            narrow(PLANE),
            narrow(planes),
            narrow(planes),
            narrow(planes),
            narrow(planes),
            singles(planes),
            singles(PLANE),
            pltpu.VMEM((size, both), jnp.float32),
            singles(),
            pltpu.VMEM((ITERS * 2, columns, 2 * columns), jnp.float32),
            pltpu.VMEM((ITERS * (peers + planes - 1), columns, 2 * columns), jnp.float32),
            pltpu.VMEM((1, devices * per_peer), jnp.int32),
            pltpu.SMEM((1, devices * per_peer), jnp.int32),
            dma((CHUNKS,)),
            dma((1,)),
            dma((len(semaphores(planes)),)),
        ],
        compiler_params=pltpu.CompilerParams(
            collective_id=0, has_side_effects=True, vmem_limit_bytes=62 * 1024 * 1024
        ),
    )(block_row[None], block_col[None], block_count, start_basis.T, kernel_blocks)
    embedded, projected = pl.pallas_call(
        functools.partial(closing, total_rows),
        out_shape=(
            jax.ShapeDtypeStruct((columns, own_rows), jnp.float32),
            jax.ShapeDtypeStruct((columns, columns), jnp.float32),
        ),
        in_specs=[vmem] * 3,
        out_specs=(vmem, vmem),
    )(image, inverse, projected)
    return embedded.T, projected


def solution(mesh):
    in_specs = (
        P(("rows", "grp"), None),
        P(("rows", "grp"), None, None),
        P(("rows", "grp")),
        P(("rows", "grp")),
        P(("rows", "grp")),
    )
    out_specs = (P(("rows", "grp"), None), P())
    return jax.shard_map(
        on_device, mesh=mesh, in_specs=in_specs, out_specs=out_specs, check_vma=False
    )
```

```python
import functools

import jax
import jax.numpy as jnp
from jax import lax
from jax.experimental import pallas as pl
from jax.experimental.pallas import tpu as pltpu
from jax.sharding import PartitionSpec as P

ITERS = 2
PLANE = 4
KINDS = 2
MESH = pl.DeviceIdType.MESH
HIGH = lax.Precision.HIGHEST
CHUNKS = 4
SPLIT_FROM = 2


def whole_diagonal(dz):
    return dz >= 3


def split_even(total, parts):
    edges = [total * i // parts for i in range(parts + 1)]
    return list(zip(edges[:-1], edges[1:]))


def nt_dot(a, b, precision=None):
    return lax.dot_general(
        a, b, (((1,), (1,)), ((), ())), preferred_element_type=jnp.float32, precision=precision
    )


def inverse_root(value):
    guess = lax.rsqrt(value)
    return guess * (1.5 - 0.5 * (value * guess) * guess)


def inverse_factor(gram, columns):
    tall = 8
    wide = 2 * columns
    row_id = lax.broadcasted_iota(jnp.int32, (columns, wide), 0)
    lane_id = lax.broadcasted_iota(jnp.int32, (columns, wide), 1)
    both = jnp.concatenate([gram, gram], axis=1)
    on_diagonal = (lane_id == row_id) | (lane_id == row_id + columns)
    diagonal = jnp.where(on_diagonal, both, 0.0)
    across = inverse_root(jnp.sum(diagonal, axis=0, keepdims=True))
    down = inverse_root(0.5 * jnp.sum(diagonal, axis=1, keepdims=True))
    unit = jnp.where(lane_id == row_id + columns, 1.0, 0.0).astype(jnp.float32)
    work = jnp.where(lane_id < columns, both * down * across, unit)
    tiles = [work[i : i + tall] for i in range(0, columns, tall)]

    def spread(row):
        return jnp.broadcast_to(row, (tall, wide))

    done = []
    for t in range(len(tiles)):
        k = t * tall
        cols = [
            [jnp.broadcast_to(tile[:, k + j : k + j + 1], (tall, wide)) for tile in tiles[t:]]
            for j in range(tall)
        ]
        rows = [spread(tiles[t][i : i + 1]) for i in range(tall)]
        p = [[spread(cols[j][0][i : i + 1]) for j in range(i + 1)] for i in range(tall)]
        inv = [None] * tall
        for j in range(0, tall, 2):
            det = p[j][j] * p[j + 1][j + 1] - p[j + 1][j] * p[j + 1][j]
            inv[j] = 1.0 / p[j][j]
            inv[j + 1] = p[j][j] * (1.0 / det)
            lead = p[j + 1][j] * inv[j]
            rows[j + 1] = rows[j + 1] - lead * rows[j]
            cols[j + 1] = [c1 - lead * c0 for c1, c0 in zip(cols[j + 1], cols[j])]
            p[j + 1][j + 1] = p[j + 1][j + 1] - lead * p[j + 1][j]
            for i in range(j + 2, tall):
                p[i][j + 1] = p[i][j + 1] - lead * p[i][j]
            for i in range(j + 2, tall):
                l0, l1 = p[i][j] * inv[j], p[i][j + 1] * inv[j + 1]
                rows[i] = rows[i] - l0 * rows[j] - l1 * rows[j + 1]
                cols[i] = [
                    ci - l0 * c0 - l1 * c1 for ci, c0, c1 in zip(cols[i], cols[j], cols[j + 1])
                ]
                for m in range(i, tall):
                    p[m][i] = p[m][i] - l0 * p[m][j] - l1 * p[m][j + 1]
        for i in range(tall):
            done.append((rows[i] * inverse_root(p[i][i]))[:1])
        scaled = [rows[i] * inv[i] for i in range(tall)]
        for at in range(t + 1, len(tiles)):
            for i in range(tall):
                tiles[at] = tiles[at] - cols[i][at - t] * scaled[i]
    return (jnp.concatenate(done, axis=0) * across)[:, columns:]


def fold(square):
    half = square.shape[0] // 2
    return jnp.concatenate([square[:half], square[half:]], axis=1)


def unfold(packed):
    half = packed.shape[1] // 2
    return jnp.concatenate([packed[:, :half], packed[:, half:]], axis=0)


def halves(dz):
    if whole_diagonal(dz):
        return ((1, 2), (1, 2))
    return ((3, 1, 2), (1, 2) if dz >= SPLIT_FROM else (3, 1, 2))


def semaphores(planes):
    far, others = range(2, planes), range(1, PLANE)
    names = ["next", "next_s"]
    for iteration in range(ITERS):
        names += [(stage + side, iteration) for stage in ("plane", "gram", "proj") for side in ("", "_s")]
    names += [("own", q) for q in others] + [("own_s", q) for q in others]
    names += [("down", q) for q in others] + [("core0", q) for q in range(PLANE)]
    names += [("core0_s", q) for q in range(PLANE)] + [("up", q) for q in range(PLANE)]
    names += [("share", q) for q in others] + [("share_s", q) for q in others]
    names += [("core", dz) for dz in range(1, planes)] + [("above_s", dz) for dz in range(1, planes)]
    names += [("pair", dz) for dz in range(planes)] + [("reduce_s", dz) for dz in range(planes)]
    for dz in far:
        names += [(name, dz) for name in ("far_s", "diag", "r_diag", "r_far")]
        names += [(name, dz, h) for name in ("far", "r_mate") for h in range(2)]
        names += [("mate", dz, q, h) for h in range(2) for q in halves(dz)[h]]
    return {name: i for i, name in enumerate(names)}


def slot_table(row_ref, col_ref, count, first_row, per_peer, places):
    slots = row_ref.shape[1]
    square = (slots, slots)
    down = lax.broadcasted_iota(jnp.int32, square, 0)
    across = lax.broadcasted_iota(jnp.int32, square, 1)
    position = lax.broadcasted_iota(jnp.int32, (1, slots), 1)

    def turn(row):
        spread = jnp.broadcast_to(row, square)
        return jnp.sum(jnp.where(down == across, spread, 0), axis=1, keepdims=True)

    target = lax.div(col_ref[...], KINDS)
    local_row = jnp.clip(row_ref[...] - first_row, 0, KINDS - 1)
    word = position * 8 + local_row * 4 + (col_ref[...] - target * KINDS) * 2 + 1
    key = jnp.where(position < count, target, -1)
    key_down, word_down = turn(key), turn(word)
    earlier = (key_down == key) & (across < down)
    rank = jnp.sum(jnp.where(earlier, 1, 0), axis=1, keepdims=True)
    spot = jnp.where(key_down >= 0, key_down * per_peer + rank, -1)
    hit = spot == lax.broadcasted_iota(jnp.int32, (slots, places), 1)
    return jnp.sum(jnp.where(hit, word_down, 0), axis=0, keepdims=True)


def kernel(
    planes, total_rows, per_peer, columns,
    row_ref, col_ref, count_ref, start_ref, blocks_hbm, embed_ref, proj_ref, inverse_ref,
    blocks, turned, gathered, pair_send, pair_recv, mate_send, mate_recv,
    up_send, up_recv, diag_send, diag_recv, far_send, far_recv, column, own_sum, forward_sum, image, line, line_recv,
    code_vector, code, load_sem, code_sem, sems,
):
    size, both = gathered.shape[1:]
    slots = blocks.shape[0]
    rows_at = lax.axis_index("rows")
    c = lax.axis_index("grp")
    z = rows_at // PLANE
    p = rows_at % PLANE
    px, py = p % 2, p // 2

    def mate(q):
        x = px + (q % 2) * (1 - 2 * px)
        y = py + (q // 2) * (1 - 2 * py)
        return 2 * y + x

    mates = [mate(q) for q in range(PLANE)]
    places = semaphores(planes)

    def sem(*name):
        return sems.at[places[name if len(name) > 1 else name[0]]]
    others = (1, 2, 3)

    def number(zz, pp, cc):
        return (zz * PLANE + pp) * 2 + cc

    def remote(src, dst, s, r, zz, pp, cc):
        return pltpu.make_async_remote_copy(
            src, dst, s, r, device_id=(zz * PLANE + pp, cc), device_id_type=MESH
        )

    loads = [
        pltpu.make_async_copy(
            blocks_hbm.at[pl.ds(lo, hi - lo)], blocks.at[pl.ds(lo, hi - lo)], load_sem.at[i]
        )
        for i, (lo, hi) in enumerate(split_even(slots, CHUNKS))
    ]
    for copy in loads:
        copy.start()
    barrier = pltpu.get_barrier_semaphore()
    greeted = [(z, mates[q], 1 - c if f else c) for q in range(PLANE) for f in (0, 1) if q or f]
    greeted += [((z + s) % planes, p, c) for s in range(1, planes)]
    for zz, pp, cc in greeted:
        pl.semaphore_signal(barrier, inc=1, device_id=(zz * PLANE + pp, cc), device_id_type=MESH)
    turned[...] = jnp.concatenate([start_ref[:, :size], start_ref[:, size:]], axis=0)
    gathered[number(z, p, c)] = turned[...].T
    code_vector[...] = slot_table(
        row_ref, col_ref, count_ref[0], number(z, p, c) * KINDS, per_peer, code_vector.shape[1]
    )
    code_copy = pltpu.make_async_copy(code_vector, code, code_sem.at[0])
    code_copy.start()
    pl.semaphore_wait(barrier, len(greeted))

    def above(dz):
        return z + dz < planes

    def below(dz):
        return z - dz >= 0

    when = pl.when
    me = number(z, p, c)

    def whole(device):
        return gathered.at[device]

    def part(device, h):
        return gathered.at[device, pl.ds(h * (size // 2), size // 2)]

    def g_next():
        at = whole(me)
        return remote(at, at, sem("next_s"), sem("next"), z - 1, p, c)

    def g_next_in():
        at = whole(number(z + 1, p, c))
        return remote(at, at, sem("next_s"), sem("next"), z + 1, p, c)

    def g_far(dz, h):
        at = part(me, h)
        return remote(at, at, sem("far_s", dz), sem("far", dz, h), z - dz, p, c)

    def g_far_in(dz, h):
        at = part(number(z + dz, p, c), h)
        return remote(at, at, sem("far_s", dz), sem("far", dz, h), z + dz, p, c)

    def g_own(q):
        at = whole(me)
        return remote(at, at, sem("own_s", q), sem("own", q), z, mates[q], c)

    def g_own_in(q):
        at = whole(number(z, mates[q], c))
        return remote(at, at, sem("own_s", q), sem("own", q), z, mates[q], c)

    def g_mate(dz, q, h):
        at = part(number(z + dz, p, c), h)
        return remote(at, at, sem("above_s", dz), sem("mate", dz, q, h), z, mates[q], c)

    def g_mate_in(dz, q, h):
        at = part(number(z + dz, mates[q], c), h)
        return remote(at, at, sem("above_s", dz), sem("mate", dz, q, h), z, mates[q], c)

    def g_down(q):
        at = whole(number(z, mates[q], c))
        return remote(at, at, sem("next_s"), sem("down", q), z - 1, p, c)

    def g_down_in(q):
        at = whole(number(z + 1, mates[q], c))
        return remote(at, at, sem("next_s"), sem("down", q), z + 1, p, c)

    def diagonal(dz, device):
        return whole(device) if whole_diagonal(dz) else part(device, 1)

    def g_diag(dz):
        at = diagonal(dz, number(z, mates[3], c))
        return remote(at, at, sem("far_s", dz), sem("diag", dz), z - dz, p, c)

    def g_diag_in(dz):
        at = diagonal(dz, number(z + dz, mates[3], c))
        return remote(at, at, sem("far_s", dz), sem("diag", dz), z + dz, p, c)

    def g_core(dz, q):
        at = whole(number(z + dz, mates[q], c))
        if dz == 0:
            pair = sem("core0_s", q), sem("core0", q)
        else:
            pair = sem("above_s", dz), sem("core", dz)
        return remote(at, at, *pair, z, p, 1 - c)

    def arrived(count, name):
        span = gathered.at[pl.ds(0, count), pl.ds(0, size // 2)]
        remote(span, span, sem(*name), sem(*name), z, p, 1 - c).wait_recv()

    def left(count, name):
        span = gathered.at[pl.ds(0, count), pl.ds(0, size // 2)]
        remote(span, span, sem(*name), sem(*name), z, p, 1 - c).wait_send()

    def down_to(q):
        return (z > 0) | (mates[q] < p)

    def up_to(q):
        return (z > 0) | (mates[q] > p)

    def r_pair(dz):
        span = pl.ds(dz * PLANE, PLANE)
        return remote(
            pair_send.at[span], pair_recv.at[span], sem("reduce_s", dz), sem("pair", dz), z, p, 1 - c
        )

    def r_own(q, h):
        at = (q, pl.ds(h * columns, columns))
        return remote(
            mate_send.at[at], mate_recv.at[at], sem("share_s", q), sem("share", q), z, mates[q], c
        )

    def r_mate(dz, q, h):
        at = (dz * PLANE + q, pl.ds(h * columns, columns))
        return remote(
            mate_send.at[at], mate_recv.at[at], sem("reduce_s", dz), sem("r_mate", dz, h), z, mates[q], c
        )

    def r_up(q):
        return remote(up_send.at[q], up_recv.at[q], sem("reduce_s", 1), sem("up", q), z + 1, p, c)

    def r_diag(dz):
        at = (dz,) if whole_diagonal(dz) else (dz, pl.ds(columns, columns))
        return remote(
            diag_send.at[at], diag_recv.at[at], sem("reduce_s", dz), sem("r_diag", dz), z + dz, p, c
        )

    def r_far(dz, h):
        at = (dz, pl.ds(h * columns, columns))
        return remote(far_send.at[at], far_recv.at[at], sem("reduce_s", dz), sem("r_far", dz), z + dz, p, c)

    def decode(word):
        return word // 8, (word // 4) % 2, (word // 2) % 2, word % 2

    nothing = jnp.zeros((columns, size), jnp.bfloat16)

    def mirror_sums(device):
        sums = None
        for j in range(per_peer):
            slot, row, col, live = decode(code[0, device * per_peer + j])
            rows = lax.select(row == 1, turned[columns:], turned[:columns])
            left = jnp.concatenate(
                [
                    lax.select(live * (1 - col) == 1, rows, nothing),
                    lax.select(live * col == 1, rows, nothing),
                ],
                axis=0,
            )
            product = jnp.dot(left, blocks[slot], preferred_element_type=jnp.float32)
            sums = product if sums is None else sums + product
        return sums

    def give(dz):
        for pp in range(PLANE):
            pair_send[dz * PLANE + pp] = mirror_sums(number(z + dz, pp, 1 - c)).astype(
                jnp.bfloat16
            )
        r_pair(dz).start()

    def keep(dz):
        r_pair(dz).wait_recv()
        for q in others + (0,):
            pp = mates[q]
            value = mirror_sums(number(z + dz, pp, c)) + pair_recv[dz * PLANE + pp].astype(
                jnp.float32
            )
            if dz == 0:
                own_sum[q] = value
            elif dz == 1:
                up_send[q] = value.astype(jnp.bfloat16)
                if q:
                    r_up(q).start()
            elif q == 0:
                column[dz] = value
            elif q == 3 and dz >= SPLIT_FROM:
                mate_send[dz * PLANE + q] = value.astype(jnp.bfloat16)
                diag_send[dz] = value.astype(jnp.bfloat16)
            else:
                mate_send[dz * PLANE + q] = value.astype(jnp.bfloat16)
        if dz >= 2:
            for h in range(2):
                for q in halves(dz)[h]:
                    r_mate(dz, q, h).start()
            if dz >= SPLIT_FROM:
                r_diag(dz).start()

    def send_own(q, h):
        at = (q, pl.ds(h * columns, columns))
        mate_send[at] = own_sum[at].astype(jnp.bfloat16)
        r_own(q, h).start()

    def pass_far(dz, h):
        at = pl.ds(h * columns, columns)
        total = column[dz, at]
        arrived(len(halves(dz)[h]), ("r_mate", dz, h))
        for q in halves(dz)[h]:
            total = total + mate_recv[dz * PLANE + q, at].astype(jnp.float32)
        far_send[dz, at] = total.astype(jnp.bfloat16)
        r_far(dz, h).start()

    lane = lax.broadcasted_iota(jnp.int32, (size, both), 1)
    sides = [
        jnp.where((lane >= columns) == bool(kind), 1.0, 0.0).astype(jnp.bfloat16)
        for kind in range(KINDS)
    ]
    neither = jnp.zeros((size, both), jnp.bfloat16)

    def forward_sums(zz, pp, lanes):
        sums = None
        for cc in lanes:
            device = number(zz, pp, cc)
            straight = gathered[device]
            crossed = jnp.concatenate([straight[:, columns:], straight[:, :columns]], axis=1)
            for j in range(per_peer):
                slot, row, col, live = decode(code[0, device * per_peer + j])
                side = lax.select(
                    live * (1 - row) == 1,
                    sides[0],
                    lax.select(live * row == 1, sides[1], neither),
                )
                right = lax.select(row == col, straight, crossed) * side
                product = jnp.dot(blocks[slot], right, preferred_element_type=jnp.float32)
                sums = product if sums is None else sums + product
        return sums

    def forward(dz, lane_at=None):
        if dz == 0:

            def one(pp, _):
                @when((z > 0) | (pp >= p))
                def _():
                    forward_sum[...] = forward_sum[...] + forward_sums(z, pp, (0, 1))

                return 0

            lax.fori_loop(0, PLANE, one, 0)
        else:
            sums = forward_sum[...]
            for pp in range(PLANE):
                sums = sums + forward_sums(z + dz, pp, (lane_at,))
            forward_sum[...] = sums

    def far_count(dz):
        return 2 + (2 if whole_diagonal(dz) else int(dz >= SPLIT_FROM))

    far = list(range(planes - 1, 1, -1))
    far_split = [dz for dz in far if dz >= SPLIT_FROM]

    for iteration in range(ITERS):
        last = iteration == ITERS - 1
        if iteration:
            gathered[me] = turned[...].T
        for h in range(2):
            for dz in far:
                when(below(dz))(lambda dz=dz, h=h: g_far(dz, h).start())
        for q in others:
            when(down_to(q))(lambda q=q: g_own(q).start())
        g_core(0, 0).start()
        forward_sum[...] = jnp.zeros_like(forward_sum)
        if iteration == 0:
            code_copy.wait()
            for copy in loads:
                copy.wait()
        order = ([1] if planes > 1 else []) + far + [0]
        steps = [("give", dz) for dz in order[:3]]
        for at, dz in enumerate(order):
            steps.append(("keep", dz))
            if at >= 1 and at + 2 < planes:
                steps.append(("give", order[at + 2]))
        for what, dz in steps:
            when(above(dz))(lambda dz=dz, what=what: (give if what == "give" else keep)(dz))
            if (what, dz) == ("keep", 1):
                when(z > 0)(lambda: g_next().start())
        if planes > 1:
            when(above(1))(lambda: r_up(0).start())

        @when(z == 0)
        def _():
            for q in others:
                for h in range(2):
                    when(up_to(q))(lambda q=q, h=h: send_own(q, h))

        for h in range(2):
            for dz in far:

                @when(above(dz))
                def _(dz=dz, h=h):
                    g_far_in(dz, h).wait_recv()
                    for q in halves(dz)[h]:
                        g_mate(dz, q, h).start()
                    if h == 1:
                        g_core(dz, 0).start()

        for q in others:

            @when(up_to(q))
            def _(q=q):
                g_own_in(q).wait_recv()

                @when(z > 0)
                def _():
                    g_down(q).start()

                if q == 3:
                    for dz in far_split:
                        when(below(dz))(lambda dz=dz: g_diag(dz).start())

                g_core(0, q).start()

        @when(z > 0)
        def _():
            for q in others:
                r_up(q).wait_recv()
                own_sum[q] = own_sum[q] + up_recv[q].astype(jnp.float32)
                early = q < 3 or not any(whole_diagonal(dz) for dz in far)
                if early:
                    send_own(q, 0)
                if q == 3:
                    for dz in far_split:

                        @when(below(dz))
                        def _(dz=dz):
                            r_diag(dz).wait_recv()
                            first = 0 if whole_diagonal(dz) else columns
                            at = pl.ds(first, 2 * columns - first)
                            own_sum[q, at] = own_sum[q, at] + diag_recv[dz, at].astype(jnp.float32)

                if not early:
                    send_own(q, 0)
                send_own(q, 1)

        for dz in far:
            for h in range(2):
                when(above(dz))(lambda dz=dz, h=h: pass_far(dz, h))

        arrived(2, ("core0", 0))
        for q in others:
            when(up_to(q))(lambda q=q: arrived(2, ("core0", q)))
        forward(0)

        if planes > 1:

            @when(above(1))
            def _():
                g_next_in().wait_recv()
                g_core(1, 0).start()
                for q in others:
                    g_down_in(q).wait_recv()
                    g_core(1, q).start()
                forward(1, c)
                arrived(2 * PLANE, ("core", 1))
                forward(1, 1 - c)

        def other_lane(dz):
            arrived(2 * PLANE, ("core", dz))
            forward(dz, 1 - c)

        for dz in far:

            @when(above(dz))
            def _(dz=dz):
                for q in others:
                    for h in range(2):
                        if q in halves(dz)[h]:
                            g_mate_in(dz, q, h).wait_recv()
                    if q == 3 and dz >= SPLIT_FROM:
                        g_diag_in(dz).wait_recv()
                    g_core(dz, q).start()
                forward(dz, c)
                if dz < planes - 1:
                    when(above(dz + 1))(lambda: other_lane(dz + 1))

        if far:
            when(above(2))(lambda: other_lane(2))

        if planes > 1:
            when(z > 0)(lambda: left(2 * PLANE, ("next_s",)))
        for dz in far:
            when(below(dz))(lambda dz=dz: left(far_count(dz), ("far_s", dz)))
        left(2, ("core0_s", 0))
        for q in others:
            when(down_to(q))(lambda q=q: left(2, ("own_s", q)))
            when(up_to(q))(lambda q=q: left(2, ("core0_s", q)))
        for dz in range(1, planes):
            count = 2 * PLANE + (len(halves(dz)[0]) + len(halves(dz)[1]) if dz >= 2 else 0)
            when(above(dz))(lambda dz=dz, count=count: left(count, ("above_s", dz)))

        image[...] = forward_sum[...].T + own_sum[0]

        @when(z > 0)
        def _():
            r_up(0).wait_recv()
            image[...] = image[...] + up_recv[0].astype(jnp.float32)

        for q in others:

            @when(down_to(q))
            def _(q=q):
                arrived(2, ("share", q))
                image[...] = image[...] + mate_recv[q].astype(jnp.float32)

        for dz in range(2, planes):

            @when(below(dz))
            def _(dz=dz):
                arrived(2, ("r_far", dz))
                image[...] = image[...] + far_recv[dz].astype(jnp.float32)

        rows = image[...]

        def diagonal_sum(square):
            return square[:columns, :columns] + square[columns:, columns:]

        gram = diagonal_sum(nt_dot(rows, rows, HIGH))
        half = columns // 2
        tall = columns if last else half
        peers = 2 * PLANE - 1
        base = iteration * 2
        rbase = iteration * (peers + planes - 1)
        line[base, :half] = fold(gram)
        if last:
            line[base, half:] = fold(diagonal_sum(nt_dot(turned[...].astype(jnp.float32), rows, HIGH)))
        copies = []
        for i, (zz, pp, cc) in enumerate(greeted[:peers]):
            copies.append(
                remote(
                    line.at[base, pl.ds(0, tall)], line_recv.at[rbase + i, pl.ds(0, tall)],
                    sem("plane_s", iteration), sem("plane", iteration), zz, pp, cc,
                )
            )
        for copy in copies:
            copy.start()
        for q in others:
            when(up_to(q))(lambda q=q: left(2, ("share_s", q)))
        for dz in range(planes):
            count = 2 * PLANE
            if dz == 1:
                count += 2 * PLANE
            if dz >= 2:
                count += len(halves(dz)[0]) + len(halves(dz)[1]) + far_count(dz)
            when(above(dz))(lambda dz=dz, count=count: left(count, ("reduce_s", dz)))

        total = line[base, :tall]
        span = line_recv.at[pl.ds(rbase, peers), pl.ds(0, tall)]
        remote(span, span, sem("plane_s", iteration), sem("plane", iteration), z, p, 1 - c).wait()
        for i in range(peers):
            total = total + line_recv[rbase + i, :tall]
        line[base + 1, :tall] = total
        def column_wait(piece):
            name = ("gram", "proj")[piece]
            span = line_recv.at[pl.ds(rbase + peers, planes - 1), pl.ds(piece * half, half)]
            remote(span, span, sem(name + "_s", iteration), sem(name, iteration), z, p, 1 - c).wait()

        for piece in range(2 if last else 1):
            span = pl.ds(piece * half, half)
            for s in range(1, planes):
                name = ("gram", "proj")[piece]
                copy = remote(
                    line.at[base + 1, span], line_recv.at[rbase + peers + s - 1, span],
                    sem(name + "_s", iteration), sem(name, iteration), (z + s) % planes, p, c,
                )
                copy.start()
        column_wait(0)
        summed = line[base + 1, :half]
        for s in range(1, planes):
            summed = summed + line_recv[rbase + peers + s - 1, :half]
        summed = unfold(summed / total_rows)
        inverse = inverse_factor(summed, columns)
        if last:
            inverse_ref[...] = inverse
            column_wait(1)
            summed = line[base + 1, half:]
            for s in range(1, planes):
                summed = summed + line_recv[rbase + peers + s - 1, half:]
            proj_ref[...] = unfold(summed)
        for kind in range(KINDS):
            at = pl.ds(kind * columns, columns)
            if last:
                embed_ref[:, kind * size : (kind + 1) * size] = image[at]
            else:
                result = jnp.dot(
                    inverse, image[at], precision=HIGH, preferred_element_type=jnp.float32
                )
                turned[at] = result.astype(jnp.bfloat16)


def closing(total_rows, image_ref, inverse_ref, sum_ref, embed_ref, proj_ref):
    embed_ref[...] = jnp.dot(
        inverse_ref[...], image_ref[...], precision=HIGH, preferred_element_type=jnp.float32
    )
    proj_ref[...] = sum_ref[...] / total_rows


def on_device(start_basis, kernel_blocks, block_row, block_col, block_count):
    devices = lax.axis_size("rows") * lax.axis_size("grp")
    slots, size, _ = kernel_blocks.shape
    own_rows, columns = start_basis.shape
    per_peer = (slots + devices - 1) // devices
    planes = lax.axis_size("rows") // PLANE
    total_rows = own_rows * devices

    smem = pl.BlockSpec(memory_space=pltpu.SMEM)
    vmem = pl.BlockSpec(memory_space=pltpu.VMEM)
    dma = pltpu.SemaphoreType.DMA
    peers = 2 * PLANE - 1
    both = KINDS * columns

    def narrow(*lead):
        return pltpu.VMEM((*lead, both, size), jnp.bfloat16)

    def singles(*lead):
        return pltpu.VMEM((*lead, both, size), jnp.float32)

    image, projected, inverse = pl.pallas_call(
        functools.partial(kernel, planes, total_rows, per_peer, columns),
        out_shape=(
            jax.ShapeDtypeStruct((columns, own_rows), jnp.float32),
            jax.ShapeDtypeStruct((columns, columns), jnp.float32),
            jax.ShapeDtypeStruct((columns, columns), jnp.float32),
        ),
        in_specs=[vmem, vmem, smem, vmem, pl.BlockSpec(memory_space=pl.ANY)],
        out_specs=(vmem, vmem, vmem),
        scratch_shapes=[
            pltpu.VMEM((slots, size, size), jnp.bfloat16),
            narrow(),
            pltpu.VMEM((devices, size, both), jnp.bfloat16),
            narrow(planes * PLANE),
            narrow(planes * PLANE),
            narrow(planes * PLANE),
            narrow(planes * PLANE),
            narrow(PLANE),
            narrow(PLANE),
            narrow(planes),
            narrow(planes),
            narrow(planes),
            narrow(planes),
            singles(planes),
            singles(PLANE),
            pltpu.VMEM((size, both), jnp.float32),
            singles(),
            pltpu.VMEM((ITERS * 2, columns, 2 * columns), jnp.float32),
            pltpu.VMEM((ITERS * (peers + planes - 1), columns, 2 * columns), jnp.float32),
            pltpu.VMEM((1, devices * per_peer), jnp.int32),
            pltpu.SMEM((1, devices * per_peer), jnp.int32),
            dma((CHUNKS,)),
            dma((1,)),
            dma((len(semaphores(planes)),)),
        ],
        compiler_params=pltpu.CompilerParams(
            collective_id=0, has_side_effects=True, vmem_limit_bytes=62 * 1024 * 1024
        ),
    )(block_row[None], block_col[None], block_count, start_basis.T, kernel_blocks)
    embedded, projected = pl.pallas_call(
        functools.partial(closing, total_rows),
        out_shape=(
            jax.ShapeDtypeStruct((columns, own_rows), jnp.float32),
            jax.ShapeDtypeStruct((columns, columns), jnp.float32),
        ),
        in_specs=[vmem] * 3,
        out_specs=(vmem, vmem),
    )(image, inverse, projected)
    return embedded.T, projected


def solution(mesh):
    in_specs = (
        P(("rows", "grp"), None),
        P(("rows", "grp"), None, None),
        P(("rows", "grp")),
        P(("rows", "grp")),
        P(("rows", "grp")),
    )
    out_specs = (P(("rows", "grp"), None), P())
    return jax.shard_map(
        on_device, mesh=mesh, in_specs=in_specs, out_specs=out_specs, check_vma=False
    )
```
